256 devices in a mesh: blk: 8 (over y_hi, x), head: 8 (over z), bend: 4 (over y_lo, core).
Axes of the slice: x: 4, y: 4 (y_hi: 2, y_lo: 2; y = y_hi * 2 + y_lo), z: 8, core: 2. Of those that a mesh axis runs over, the one named last changes fastest.
Arguments:
- queries: bfloat16 [65536, 768], P(('bend', 'blk', 'head')), parts along dimension 0, may hold values from -9 to 9
- keys_values: bfloat16 [2, 65536, 768], P(None, ('bend', 'blk', 'head')), parts along dimension 1, may hold values from -6 to 6
- surface: bfloat16 [65536, 768], P(('bend', 'blk', 'head')), parts along dimension 0, may hold values from -6 to 6
- out_weight: bfloat16 [768, 768], P('head'), may hold values from -0.21875 to 0.21875
- up_weight: bfloat16 [768, 3072], P('head'), may hold values from -0.21875 to 0.21875
- down_weight: bfloat16 [3072, 768], P('head'), may hold values from -0.109375 to 0.109375
- norm_gain: float32 [768], replicated, may hold values from 0.25 to 1.75
- block_lists: int32 [256, 4], P(('bend', 'blk', 'head')), parts along dimension 0, may hold values from 0 to 63, as said below
- list_lengths: int32 [256], P(('bend', 'blk', 'head')), parts along dimension 0, may hold values from 1 to 4
Outputs:
- mixed_out: bfloat16 [65536, 768], P(('bend', 'blk', 'head')), parts along dimension 0
The draws below stay inside these ranges and needn't reach their ends.
There are 4 independent parts, one for each index of `bend`. The reference program is written for one: setup_inputs(seed, part) draws one part's arguments, and reference() takes and returns one part's arrays. A program takes and returns all parts, laid end to end along the dimension named above; an argument that names none is the same for every part. Nothing has to cross between parts.
Inputs may be any that keep to these rules, and one draw needn't show every extreme that they name: `block_lists`: the list of query block b holds distinct anchor blocks, all within cycle distance 3 (modulo 64) of anchor block b, and its first entry is that block itself.
All inputs are finite; a program needn't handle non-finite values.
Results may differ from the reference program's by a relative error of at most 0.0065.
Values may be sent and summed in bfloat16 or wider, within the bound.
A program may use at most 128 MiB of HBM per device.

```python
import jax
import jax.numpy as jnp
from jax import lax

D = 768
HEADS = 12
HD = 64
FF = 3072
BLOCK = 256
LIST = 4
QB_DEV = 1
ANCHOR_BLOCKS = 64
REACH = 3
NQB = 64
NQ = 16384
NA = 16384


def draw_queries(key, part):
    drawn_key = jax.random.fold_in(key, 21)
    drawn = jnp.clip(jax.random.normal(drawn_key, (NQ, D), jnp.float32), -6.0, 6.0)
    return drawn.astype(jnp.bfloat16)


def draw_keys_values(key, part):
    drawn_key = jax.random.fold_in(key, 31)
    drawn = jnp.clip(jax.random.normal(drawn_key, (2, NA, D), jnp.float32), -6.0, 6.0)
    return drawn.astype(jnp.bfloat16)


def draw_block_lists(key, part):
    drawn_key = jax.random.fold_in(key, 41)
    candidates = 2 * REACH
    tickets = jax.random.randint(drawn_key, (NQB, candidates), 0, 2 ** 20) * candidates + jnp.arange(candidates)[None, :]
    picked = jnp.argsort(tickets, axis=1)[:, :LIST - 1]
    offsets = jnp.where(picked < REACH, picked - REACH, picked - REACH + 1)
    home_block = jnp.arange(NQB) // QB_DEV
    others = (home_block[:, None] + offsets) % ANCHOR_BLOCKS
    return jnp.concatenate([home_block[:, None], others], axis=1).astype(jnp.int32)


def draw_list_lengths(key, part):
    drawn_key = jax.random.fold_in(key, 51)
    lengths = jax.random.randint(drawn_key, (NQB,), 1, LIST + 1)
    return lengths.at[0].set(LIST).at[1].set(1).astype(jnp.int32)


def level_of(own_key, extent, shards, smallest, high):
    loudness, own = 1.0, jax.random.fold_in(own_key, 6)
    for dim, blocks in shards:
        steps = jnp.exp(jax.random.uniform(jax.random.fold_in(own, dim), (blocks,), jnp.float32, smallest / len(shards), high / len(shards)))
        loudness = loudness * jnp.repeat(steps, extent[dim] // blocks).reshape([-1 if axis == dim else 1 for axis in range(len(extent))])
    return loudness


def centred(key, dims, width, reach, pieces=(), kind=jnp.bfloat16):
    values = jax.random.normal(key, dims, jnp.float32) * width
    if len(pieces) > 0:
        values = level_of(key, dims, pieces, -0.22, 0.18) * values
    return jnp.clip(values, min=-reach, max=reach).astype(kind)


def setup_inputs(seed: int = 0, part: int = 0) -> dict:
    key_list = jax.random.split(jax.random.key(seed), 10)
    part_splits = jax.random.split(jax.random.fold_in(key_list[9], part), 10)
    return {
        "queries": draw_queries(jax.random.fold_in(jax.random.fold_in(key_list[9], part), 71), part),
        "keys_values": draw_keys_values(jax.random.fold_in(jax.random.fold_in(key_list[9], part), 71), part),
        "surface": centred(part_splits[2], (NQ, D), 1.0, 6.0, ((0, 64),)),
        "out_weight": centred(key_list[3], (D, D), D ** -0.5, 0.21875, ((0, 8),)),
        "up_weight": centred(key_list[4], (D, FF), D ** -0.5, 0.21875, ((0, 8),)),
        "down_weight": centred(key_list[5], (FF, D), FF ** -0.5, 0.109375, ((0, 8),)),
        "norm_gain": jnp.clip(1.0 + 0.15 * jax.random.normal(key_list[6], (D,), jnp.float32), 0.25, 1.75),
        "block_lists": draw_block_lists(jax.random.fold_in(jax.random.fold_in(key_list[9], part), 71), part),
        "list_lengths": draw_list_lengths(jax.random.fold_in(jax.random.fold_in(key_list[9], part), 71), part),
    }


def reference(queries, keys_values, surface, out_weight, up_weight, down_weight, norm_gain, block_lists, list_lengths):
    anchor_keys = keys_values[0].reshape(ANCHOR_BLOCKS, BLOCK, HEADS, HD)
    anchor_values = keys_values[1].reshape(ANCHOR_BLOCKS, BLOCK, HEADS, HD)
    query_blocks = queries.reshape(NQB, BLOCK, HEADS, HD)

    def one_block(inputs):
        query_block, anchor_ids, live_count = inputs
        picked_keys = anchor_keys[anchor_ids].astype(jnp.float32)
        picked_values = anchor_values[anchor_ids].astype(jnp.float32)
        scores = jnp.einsum('qhd,lkhd->hqlk', query_block.astype(jnp.float32), picked_keys) * (1.0 / HD ** 0.5)
        live_mask = jnp.arange(LIST, dtype=jnp.int32) < live_count
        scores = jnp.where(live_mask[None, None, :, None], scores, -jnp.inf)
        row_max = lax.optimization_barrier(jnp.max(scores, axis=(2, 3), keepdims=True))
        weights_exp = jnp.exp(scores - row_max)
        row_total = lax.optimization_barrier(jnp.sum(weights_exp, axis=(2, 3)))
        probs = weights_exp.astype(jnp.bfloat16)
        context = jnp.einsum('hqlk,lkhd->qhd', probs.astype(jnp.float32), picked_values)
        context = context / jnp.transpose(row_total)[:, :, None]
        return context.reshape(BLOCK, D).astype(jnp.bfloat16)
    context = lax.map(one_block, (query_blocks, block_lists, list_lengths)).reshape(NQ, D)
    hidden = surface.astype(jnp.float32) + jnp.dot(context, out_weight, preferred_element_type=jnp.float32)
    mean_square = lax.optimization_barrier(jnp.mean(hidden * hidden, axis=1, keepdims=True))
    normed = (hidden * lax.rsqrt(mean_square + 1e-05) * norm_gain[None, :]).astype(jnp.bfloat16)
    activated = jax.nn.gelu(jnp.dot(normed, up_weight, preferred_element_type=jnp.float32), approximate=True).astype(jnp.bfloat16)
    mixed_out = hidden + jnp.dot(activated, down_weight, preferred_element_type=jnp.float32)
    return mixed_out.astype(jnp.bfloat16)
```

```python
import functools

import jax
import jax.numpy as jnp
from jax import lax
from jax.experimental import pallas as pl
from jax.experimental.pallas import tpu as pltpu
from jax.sharding import PartitionSpec as P

HEADS = 12
HD = 64
LIST = 4
REACH = 3


def ring_shift(block, axis, size, distance):
    route = [(i, (i + distance) % size) for i in range(size)]
    return lax.ppermute(block, axis, route)


def x_shift(block, blk_size, x_size, distance):
    route = []
    for i in range(blk_size):
        hi, x = divmod(i, x_size)
        route.append((i, hi * x_size + (x + distance) % x_size))
    return lax.ppermute(block, "blk", route)


def core_swap(block, bend_size):
    route = [(i, i ^ 1) for i in range(bend_size)]
    return lax.ppermute(block, "bend", route)


def attention_kernel(n_blocks, mask_ref, q_ref, *refs):
    kv_refs = refs[:n_blocks]
    o_ref = refs[n_blocks]
    s_scr, m_scr, l_scr, acc_scr = refs[n_blocks + 1:]
    rows = q_ref.shape[0]
    for hh in range(2):
        cols = slice(hh * HD, (hh + 1) * HD)
        qh = q_ref[:, cols]
        m_scr[...] = jnp.full(m_scr.shape, -jnp.inf, jnp.float32)
        l_scr[...] = jnp.zeros(l_scr.shape, jnp.float32)
        acc_scr[...] = jnp.zeros(acc_scr.shape, jnp.float32)
        for j in range(n_blocks):
            @pl.when(mask_ref[j] > 0)
            def _():
                kh = kv_refs[j][0, :, cols]
                s = lax.dot_general(qh, kh, (((1,), (1,)), ((), ())),
                                    preferred_element_type=jnp.float32) * (1.0 / HD**0.5)
                s_scr[j] = s
                m_scr[...] = jnp.maximum(m_scr[...], jnp.max(s, axis=1, keepdims=True))
        for j in range(n_blocks):
            @pl.when(mask_ref[j] > 0)
            def _():
                w = jnp.exp(s_scr[j] - m_scr[...])
                l_scr[...] += jnp.sum(w, axis=1, keepdims=True)
                vh = kv_refs[j][1, :, cols]
                acc_scr[...] += jnp.dot(w.astype(jnp.bfloat16), vh,
                                        preferred_element_type=jnp.float32)
        o_ref[:, cols] = (acc_scr[...] / l_scr[...]).astype(o_ref.dtype)
    del rows


def attend(mask, q, blocks):
    rows, width = q.shape
    n_blocks = len(blocks)
    pair = 2 * HD
    grid_spec = pltpu.PrefetchScalarGridSpec(
        num_scalar_prefetch=1,
        grid=(width // pair,),
        in_specs=[pl.BlockSpec((rows, pair), lambda p, m: (0, p))]
        + [pl.BlockSpec((2, rows, pair), lambda p, m: (0, 0, p))] * n_blocks,
        out_specs=pl.BlockSpec((rows, pair), lambda p, m: (0, p)),
        scratch_shapes=[
            pltpu.VMEM((n_blocks, rows, rows), jnp.float32),
            pltpu.VMEM((rows, 1), jnp.float32),
            pltpu.VMEM((rows, 1), jnp.float32),
            pltpu.VMEM((rows, HD), jnp.float32),
        ],
    )
    return pl.pallas_call(
        functools.partial(attention_kernel, n_blocks),
        grid_spec=grid_spec,
        out_shape=jax.ShapeDtypeStruct((rows, width), jnp.bfloat16),
        cost_estimate=pl.CostEstimate(
            flops=4 * rows * rows * width * n_blocks,
            transcendentals=rows * rows * HEADS * n_blocks,
            bytes_accessed=2 * rows * width * (2 * n_blocks + 2),
        ),
    )(mask, q, *blocks)


def gather_weight_pieces(pieces, blk_size, x_size, bend_size, x, core):
    gathered = tuple(lax.all_gather(w, "head", axis=0, tiled=True) for w in pieces)
    from_left = x_shift(gathered, blk_size, x_size, 1)
    from_right = x_shift(gathered, blk_size, x_size, -1)
    tops = tuple(w[: w.shape[0] // 2] for w in from_left)
    bottoms = tuple(w[w.shape[0] // 2:] for w in from_right)
    far_top = x_shift(tops, blk_size, x_size, 1)
    far_bottom = x_shift(bottoms, blk_size, x_size, -1)
    far = tuple(jnp.concatenate([a, b], axis=0) for a, b in zip(far_top, far_bottom))
    mine = (gathered, from_left, from_right, far)
    partner = core_swap(mine, bend_size)
    absolute = jnp.arange(2 * x_size, dtype=jnp.int32)
    abs_x, abs_c = absolute // 2, absolute % 2
    dx = (abs_x - x) % x_size
    dxi = jnp.array([0, 2, 3, 1], jnp.int32)[dx]
    order = (abs_c ^ core) * 4 + dxi
    full = []
    for k in range(len(pieces)):
        stack = jnp.stack([mine[i][k] for i in range(4)] + [partner[i][k] for i in range(4)])
        stack = jnp.take(stack, order, axis=0)
        n, r, c = stack.shape
        full.append(jnp.transpose(stack, (1, 0, 2)).reshape(r, n * c))
    return full


def shards(
    queries,
    keys_values,
    surface,
    out_weight,
    up_weight,
    down_weight,
    norm_gain,
    block_lists,
    list_lengths,
):
    row_count, feature_width = queries.shape
    loop_size = lax.axis_size(("blk", "head"))
    blk_size = lax.axis_size("blk")
    bend_size = lax.axis_size("bend")
    x_size = 4
    own_index = lax.axis_index(("blk", "head"))
    x = lax.axis_index("blk") % x_size
    core = lax.axis_index("bend") % 2
    piece = x * 2 + core
    n_pieces = 2 * x_size

    def cols(w):
        width = w.shape[1] // n_pieces
        return lax.dynamic_slice_in_dim(w, piece * width, width, axis=1)

    out_full, up_full, down_full = gather_weight_pieces(
        (cols(out_weight), cols(up_weight), cols(down_weight)),
        blk_size, x_size, bend_size, x, core)

    blocks = [keys_values]
    ids = [own_index]
    left = right = keys_values
    for d in range(1, REACH + 1):
        left = ring_shift(left, ("blk", "head"), loop_size, 1)
        right = ring_shift(right, ("blk", "head"), loop_size, -1)
        blocks += [left, right]
        ids += [(own_index - d) % loop_size, (own_index + d) % loop_size]
    entry_live = jnp.arange(LIST, dtype=jnp.int32) < list_lengths[0]
    mask = jnp.stack(
        [jnp.any((block_lists[0] == b) & entry_live) for b in ids]).astype(jnp.int32)
    context = attend(mask, queries, blocks)

    hidden = surface.astype(jnp.float32) + jnp.dot(
        context, out_full, preferred_element_type=jnp.float32)
    mean_square = jnp.mean(hidden * hidden, axis=1, keepdims=True)
    normed = (hidden * lax.rsqrt(mean_square + 1e-05) * norm_gain[None, :]).astype(jnp.bfloat16)
    pre_gelu = jnp.dot(normed, up_full, preferred_element_type=jnp.float32)
    activated = jax.nn.gelu(pre_gelu, approximate=True).astype(jnp.bfloat16)
    mixed_out = hidden + jnp.dot(activated, down_full, preferred_element_type=jnp.float32)
    return mixed_out.astype(jnp.bfloat16)


def solution(mesh):
    return jax.shard_map(
        shards,
        mesh=mesh,
        in_specs=(
            P(("bend", "blk", "head"), None),
            P(None, ("bend", "blk", "head"), None),
            P(("bend", "blk", "head"), None),
            P("head", None),
            P("head", None),
            P("head", None),
            P(),
            P(("bend", "blk", "head"), None),
            P(("bend", "blk", "head")),
        ),
        out_specs=P(("bend", "blk", "head"), None),
        check_vma=False,
    )
```

```python
import functools

import jax
import jax.numpy as jnp
from jax import lax
from jax.experimental import pallas as pl
from jax.experimental.pallas import tpu as pltpu
from jax.sharding import PartitionSpec as P

HEADS = 12
HD = 64
LIST = 4
REACH = 3


def ring_shift(block, axis, size, distance):
    route = [(i, (i + distance) % size) for i in range(size)]
    return lax.ppermute(block, axis, route)


def x_shift(block, blk_size, x_size, distance):
    route = []
    for i in range(blk_size):
        hi, x = divmod(i, x_size)
        route.append((i, hi * x_size + (x + distance) % x_size))
    return lax.ppermute(block, "blk", route)


def core_swap(block, bend_size):
    route = [(i, i ^ 1) for i in range(bend_size)]
    return lax.ppermute(block, "bend", route)


def attention_kernel(n_blocks, mask_ref, q_ref, *refs):
    kv_refs = refs[:n_blocks]
    o_ref = refs[n_blocks]
    m_scr, l_scr, acc_scr = refs[n_blocks + 1:]
    scale = 1.0 / HD**0.5
    q = q_ref[...]
    first = lax.broadcasted_iota(jnp.int32, q.shape, 1) < HD
    zero = jnp.zeros_like(q)
    halves = (jnp.where(first, q, zero), jnp.where(first, zero, q))
    for hh, qh in enumerate(halves):
        m_scr[hh] = jnp.full(m_scr.shape[1:], -jnp.inf, jnp.float32)
        l_scr[hh] = jnp.zeros(l_scr.shape[1:], jnp.float32)
        acc_scr[hh] = jnp.zeros(acc_scr.shape[1:], jnp.float32)
        for j in range(n_blocks):
            @pl.when(mask_ref[j] > 0)
            def _():
                s = lax.dot_general(qh, kv_refs[j][0], (((1,), (1,)), ((), ())),
                                    preferred_element_type=jnp.float32) * scale
                m_scr[hh] = jnp.maximum(m_scr[hh], jnp.max(s, axis=1, keepdims=True))
        for j in range(n_blocks):
            @pl.when(mask_ref[j] > 0)
            def _():
                s = lax.dot_general(qh, kv_refs[j][0], (((1,), (1,)), ((), ())),
                                    preferred_element_type=jnp.float32) * scale
                w = jnp.exp(s - m_scr[hh])
                l_scr[hh] += jnp.sum(w, axis=1, keepdims=True)
                acc_scr[hh] += jnp.dot(w.astype(jnp.bfloat16), kv_refs[j][1],
                                       preferred_element_type=jnp.float32)
    lane = lax.broadcasted_iota(jnp.int32, acc_scr.shape[1:], 1) < HD
    o_ref[...] = jnp.where(lane, acc_scr[0] / l_scr[0], acc_scr[1] / l_scr[1]).astype(o_ref.dtype)


def attend(mask, q, blocks):
    rows, width = q.shape
    n_blocks = len(blocks)
    pair = 2 * HD
    grid_spec = pltpu.PrefetchScalarGridSpec(
        num_scalar_prefetch=1,
        grid=(width // pair,),
        in_specs=[pl.BlockSpec((rows, pair), lambda p, m: (0, p))]
        + [pl.BlockSpec((2, rows, pair), lambda p, m: (0, 0, p))] * n_blocks,
        out_specs=pl.BlockSpec((rows, pair), lambda p, m: (0, p)),
        scratch_shapes=[
            pltpu.VMEM((2, rows, 1), jnp.float32),
            pltpu.VMEM((2, rows, 1), jnp.float32),
            pltpu.VMEM((2, rows, pair), jnp.float32),
        ],
    )
    return pl.pallas_call(
        functools.partial(attention_kernel, n_blocks),
        grid_spec=grid_spec,
        out_shape=jax.ShapeDtypeStruct((rows, width), jnp.bfloat16),
        cost_estimate=pl.CostEstimate(
            flops=12 * rows * rows * width * 4,
            transcendentals=rows * rows * HEADS * 4,
            bytes_accessed=2 * rows * width * (2 * n_blocks + 2),
        ),
    )(mask, q, *blocks)


def order_of(offsets, me, n):
    held = (me + jnp.array(offsets, jnp.int32)) % n
    return jnp.argmax(held[None, :] == jnp.arange(n, dtype=jnp.int32)[:, None], axis=1)


def split_halves(tree, take_first):
    return tuple(w[: w.shape[0] // 2] if take_first else w[w.shape[0] // 2:] for w in tree)


def gather_over_head(pieces, n):
    me = lax.axis_index("head")
    rel, offsets = [pieces], [0]
    left = right = pieces
    for k in range(1, n // 2):
        left = ring_shift(left, "head", n, 1)
        right = ring_shift(right, "head", n, -1)
        rel += [left, right]
        offsets += [-k, k]
    far_top = ring_shift(split_halves(left, True), "head", n, 1)
    far_bottom = ring_shift(split_halves(right, False), "head", n, -1)
    rel.append(tuple(jnp.concatenate([a, b], axis=0) for a, b in zip(far_top, far_bottom)))
    offsets.append(n // 2)
    order = order_of(offsets, me, n)
    return tuple(jnp.take(jnp.stack([r[k] for r in rel]), order, axis=0)
                 for k in range(len(pieces)))


def gather_over_x_and_core(pieces, blk_size, x_size, bend_size, x, core):
    from_left = x_shift(pieces, blk_size, x_size, 1)
    from_right = x_shift(pieces, blk_size, x_size, -1)
    far_top = x_shift(split_halves(from_left, True), blk_size, x_size, 1)
    far_bottom = x_shift(split_halves(from_right, False), blk_size, x_size, -1)
    far = tuple(jnp.concatenate([a, b], axis=0) for a, b in zip(far_top, far_bottom))
    mine = (pieces, from_left, from_right, far)
    partner = core_swap(mine, bend_size)
    absolute = jnp.arange(2 * x_size, dtype=jnp.int32)
    abs_x, abs_c = absolute // 2, absolute % 2
    dx = (abs_x - x) % x_size
    dxi = jnp.array([0, 2, 3, 1], jnp.int32)[dx]
    order = (abs_c ^ core) * 4 + dxi
    return tuple(
        jnp.take(jnp.stack([mine[i][k] for i in range(4)] + [partner[i][k] for i in range(4)]),
                 order, axis=0)
        for k in range(len(pieces)))


def shards(
    queries,
    keys_values,
    surface,
    out_weight,
    up_weight,
    down_weight,
    norm_gain,
    block_lists,
    list_lengths,
):
    row_count, feature_width = queries.shape
    loop_size = lax.axis_size(("blk", "head"))
    blk_size = lax.axis_size("blk")
    bend_size = lax.axis_size("bend")
    x_size = 4
    own_index = lax.axis_index(("blk", "head"))
    x = lax.axis_index("blk") % x_size
    core = lax.axis_index("bend") % 2
    piece = x * 2 + core
    n_pieces = 2 * x_size

    head_size = lax.axis_size("head")
    out_rows = out_weight.shape[0] // n_pieces
    down_rows = down_weight.shape[0] // n_pieces
    up_cols = up_weight.shape[1] // n_pieces
    pieces = (
        lax.dynamic_slice_in_dim(out_weight, piece * out_rows, out_rows, axis=0),
        lax.dynamic_slice_in_dim(up_weight, piece * up_cols, up_cols, axis=1),
        lax.dynamic_slice_in_dim(down_weight, piece * down_rows, down_rows, axis=0),
    )
    out_z, up_z, down_z = gather_over_head(pieces, head_size)
    up_z = up_z.reshape(-1, up_cols)
    out_p, up_p, down_p = gather_over_x_and_core(
        (out_z, up_z, down_z), blk_size, x_size, bend_size, x, core)
    d = feature_width
    out_full = jnp.transpose(out_p, (1, 0, 2, 3)).reshape(d, d)
    up_full = jnp.transpose(up_p, (1, 0, 2)).reshape(d, n_pieces * up_cols)
    down_full = jnp.transpose(down_p, (1, 0, 2, 3)).reshape(-1, d)

    blocks = [keys_values]
    ids = [own_index]
    left = right = keys_values
    for d in range(1, REACH + 1):
        left = ring_shift(left, ("blk", "head"), loop_size, 1)
        right = ring_shift(right, ("blk", "head"), loop_size, -1)
        blocks += [left, right]
        ids += [(own_index - d) % loop_size, (own_index + d) % loop_size]
    entry_live = jnp.arange(LIST, dtype=jnp.int32) < list_lengths[0]
    mask = jnp.stack(
        [jnp.any((block_lists[0] == b) & entry_live) for b in ids]).astype(jnp.int32)
    context = attend(mask, queries, blocks)

    hidden = surface.astype(jnp.float32) + jnp.dot(
        context, out_full, preferred_element_type=jnp.float32)
    mean_square = jnp.mean(hidden * hidden, axis=1, keepdims=True)
    normed = (hidden * lax.rsqrt(mean_square + 1e-05) * norm_gain[None, :]).astype(jnp.bfloat16)
    pre_gelu = jnp.dot(normed, up_full, preferred_element_type=jnp.float32)
    activated = jax.nn.gelu(pre_gelu, approximate=True).astype(jnp.bfloat16)
    mixed_out = hidden + jnp.dot(activated, down_full, preferred_element_type=jnp.float32)
    return mixed_out.astype(jnp.bfloat16)


def solution(mesh):
    return jax.shard_map(
        shards,
        mesh=mesh,
        in_specs=(
            P(("bend", "blk", "head"), None),
            P(None, ("bend", "blk", "head"), None),
            P(("bend", "blk", "head"), None),
            P("head", None),
            P("head", None),
            P("head", None),
            P(),
            P(("bend", "blk", "head"), None),
            P(("bend", "blk", "head")),
        ),
        out_specs=P(("bend", "blk", "head"), None),
        check_vma=False,
    )
```

```python
import functools

import jax
import jax.numpy as jnp
from jax import lax
from jax.experimental import pallas as pl
from jax.experimental.pallas import tpu as pltpu
from jax.sharding import PartitionSpec as P

HEADS = 12
HD = 64
LIST = 4
REACH = 3


def ring_shift(block, axis, size, distance):
    route = [(i, (i + distance) % size) for i in range(size)]
    return lax.ppermute(block, axis, route)


def x_shift(block, blk_size, x_size, distance):
    route = []
    for i in range(blk_size):
        hi, x = divmod(i, x_size)
        route.append((i, hi * x_size + (x + distance) % x_size))
    return lax.ppermute(block, "blk", route)


def core_swap(block, bend_size):
    route = [(i, i ^ 1) for i in range(bend_size)]
    return lax.ppermute(block, "bend", route)


def attention_kernel(n_blocks, mask_ref, q_ref, *refs):
    kv_refs = refs[:n_blocks]
    o_ref = refs[n_blocks]
    m_scr, l_scr, acc_scr = refs[n_blocks + 1:]
    scale = 1.0 / HD**0.5
    q_t = q_ref[...].T
    first = lax.broadcasted_iota(jnp.int32, q_t.shape, 0) < HD
    zero = jnp.zeros_like(q_t)
    halves = (jnp.where(first, q_t, zero), jnp.where(first, zero, q_t))
    for hh in range(2):
        m_scr[hh] = jnp.full(m_scr.shape[1:], -jnp.inf, jnp.float32)
        l_scr[hh] = jnp.zeros(l_scr.shape[1:], jnp.float32)
        acc_scr[hh] = jnp.zeros(acc_scr.shape[1:], jnp.float32)
    for j in range(n_blocks):
        @pl.when(mask_ref[j] > 0)
        def _():
            k = kv_refs[j][0]
            for hh in range(2):
                s_t = jnp.dot(k, halves[hh], preferred_element_type=jnp.float32) * scale
                m_scr[hh] = jnp.maximum(m_scr[hh], jnp.max(s_t, axis=0, keepdims=True))
    for j in range(n_blocks):
        @pl.when(mask_ref[j] > 0)
        def _():
            k = kv_refs[j][0]
            v_t = kv_refs[j][1].T
            for hh in range(2):
                s_t = jnp.dot(k, halves[hh], preferred_element_type=jnp.float32) * scale
                w_t = jnp.exp(s_t - m_scr[hh])
                l_scr[hh] += jnp.sum(w_t, axis=0, keepdims=True)
                acc_scr[hh] += jnp.dot(v_t, w_t.astype(jnp.bfloat16),
                                       preferred_element_type=jnp.float32)
    lane = lax.broadcasted_iota(jnp.int32, acc_scr.shape[1:], 0) < HD
    out_t = jnp.where(lane, acc_scr[0] / l_scr[0], acc_scr[1] / l_scr[1])
    o_ref[...] = out_t.T.astype(o_ref.dtype)


def attend(mask, q, blocks):
    rows, width = q.shape
    n_blocks = len(blocks)
    pair = 2 * HD
    grid_spec = pltpu.PrefetchScalarGridSpec(
        num_scalar_prefetch=1,
        grid=(width // pair,),
        in_specs=[pl.BlockSpec((rows, pair), lambda p, m: (0, p))]
        + [pl.BlockSpec((2, rows, pair), lambda p, m: (0, 0, p))] * n_blocks,
        out_specs=pl.BlockSpec((rows, pair), lambda p, m: (0, p)),
        scratch_shapes=[
            pltpu.VMEM((2, 1, rows), jnp.float32),
            pltpu.VMEM((2, 1, rows), jnp.float32),
            pltpu.VMEM((2, pair, rows), jnp.float32),
        ],
    )
    return pl.pallas_call(
        functools.partial(attention_kernel, n_blocks),
        grid_spec=grid_spec,
        out_shape=jax.ShapeDtypeStruct((rows, width), jnp.bfloat16),
        cost_estimate=pl.CostEstimate(
            flops=12 * rows * rows * width * 4,
            transcendentals=rows * rows * HEADS * 4,
            bytes_accessed=2 * rows * width * (2 * n_blocks + 2),
        ),
    )(mask, q, *blocks)


def order_of(offsets, me, n):
    held = (me + jnp.array(offsets, jnp.int32)) % n
    return jnp.argmax(held[None, :] == jnp.arange(n, dtype=jnp.int32)[:, None], axis=1)


def split_halves(tree, take_first):
    return tuple(w[: w.shape[0] // 2] if take_first else w[w.shape[0] // 2:] for w in tree)


def gather_over_head(pieces, n):
    me = lax.axis_index("head")
    rel, offsets = [pieces], [0]
    left = right = pieces
    for k in range(1, n // 2):
        left = ring_shift(left, "head", n, 1)
        right = ring_shift(right, "head", n, -1)
        rel += [left, right]
        offsets += [-k, k]
    far_top = ring_shift(split_halves(left, True), "head", n, 1)
    far_bottom = ring_shift(split_halves(right, False), "head", n, -1)
    rel.append(tuple(jnp.concatenate([a, b], axis=0) for a, b in zip(far_top, far_bottom)))
    offsets.append(n // 2)
    order = order_of(offsets, me, n)
    return tuple(jnp.take(jnp.stack([r[k] for r in rel]), order, axis=0)
                 for k in range(len(pieces)))


def gather_over_x_and_core(pieces, blk_size, x_size, bend_size, x, core):
    from_left = x_shift(pieces, blk_size, x_size, 1)
    from_right = x_shift(pieces, blk_size, x_size, -1)
    far_top = x_shift(split_halves(from_left, True), blk_size, x_size, 1)
    far_bottom = x_shift(split_halves(from_right, False), blk_size, x_size, -1)
    far = tuple(jnp.concatenate([a, b], axis=0) for a, b in zip(far_top, far_bottom))
    mine = (pieces, from_left, from_right, far)
    partner = core_swap(mine, bend_size)
    absolute = jnp.arange(2 * x_size, dtype=jnp.int32)
    abs_x, abs_c = absolute // 2, absolute % 2
    dx = (abs_x - x) % x_size
    dxi = jnp.array([0, 2, 3, 1], jnp.int32)[dx]
    order = (abs_c ^ core) * 4 + dxi
    return tuple(
        jnp.take(jnp.stack([mine[i][k] for i in range(4)] + [partner[i][k] for i in range(4)]),
                 order, axis=0)
        for k in range(len(pieces)))


def shards(
    queries,
    keys_values,
    surface,
    out_weight,
    up_weight,
    down_weight,
    norm_gain,
    block_lists,
    list_lengths,
):
    row_count, feature_width = queries.shape
    loop_size = lax.axis_size(("blk", "head"))
    blk_size = lax.axis_size("blk")
    bend_size = lax.axis_size("bend")
    x_size = 4
    own_index = lax.axis_index(("blk", "head"))
    x = lax.axis_index("blk") % x_size
    core = lax.axis_index("bend") % 2
    piece = x * 2 + core
    n_pieces = 2 * x_size

    out_rows = out_weight.shape[0] // n_pieces
    down_rows = down_weight.shape[0] // n_pieces
    up_cols = up_weight.shape[1] // n_pieces
    pieces = (
        lax.dynamic_slice_in_dim(out_weight, piece * out_rows, out_rows, axis=0),
        lax.dynamic_slice_in_dim(up_weight, piece * up_cols, up_cols, axis=1),
        lax.dynamic_slice_in_dim(down_weight, piece * down_rows, down_rows, axis=0),
    )
    sizes = [w.size for w in pieces]
    packed = jnp.concatenate([w.reshape(-1) for w in pieces])
    by_head = lax.all_gather(packed, "head", axis=0, tiled=False)
    (all_pieces,) = gather_over_x_and_core(
        (by_head,), blk_size, x_size, bend_size, x, core)
    n_heads = by_head.shape[0]
    d = feature_width
    o0, o1 = sizes[0], sizes[0] + sizes[1]
    out_full = jnp.transpose(
        all_pieces[:, :, :o0].reshape(n_pieces, n_heads, out_rows, d), (1, 0, 2, 3)).reshape(d, d)
    up_full = jnp.transpose(
        all_pieces[:, :, o0:o1].reshape(n_pieces, n_heads, -1, up_cols), (1, 2, 0, 3)
    ).reshape(d, n_pieces * up_cols)
    down_full = jnp.transpose(
        all_pieces[:, :, o1:].reshape(n_pieces, n_heads, down_rows, d), (1, 0, 2, 3)
    ).reshape(-1, d)

    blocks = [keys_values]
    ids = [own_index]
    left = right = keys_values
    for d in range(1, REACH + 1):
        left = ring_shift(left, ("blk", "head"), loop_size, 1)
        right = ring_shift(right, ("blk", "head"), loop_size, -1)
        blocks += [left, right]
        ids += [(own_index - d) % loop_size, (own_index + d) % loop_size]
    entry_live = jnp.arange(LIST, dtype=jnp.int32) < list_lengths[0]
    mask = jnp.stack(
        [jnp.any((block_lists[0] == b) & entry_live) for b in ids]).astype(jnp.int32)
    context = attend(mask, queries, blocks)

    hidden = surface.astype(jnp.float32) + jnp.dot(
        context, out_full, preferred_element_type=jnp.float32)
    mean_square = jnp.mean(hidden * hidden, axis=1, keepdims=True)
    normed = (hidden * lax.rsqrt(mean_square + 1e-05) * norm_gain[None, :]).astype(jnp.bfloat16)
    pre_gelu = jnp.dot(normed, up_full, preferred_element_type=jnp.float32)
    activated = jax.nn.gelu(pre_gelu, approximate=True).astype(jnp.bfloat16)
    mixed_out = hidden + jnp.dot(activated, down_full, preferred_element_type=jnp.float32)
    return mixed_out.astype(jnp.bfloat16)


def solution(mesh):
    return jax.shard_map(
        shards,
        mesh=mesh,
        in_specs=(
            P(("bend", "blk", "head"), None),
            P(None, ("bend", "blk", "head"), None),
            P(("bend", "blk", "head"), None),
            P("head", None),
            P("head", None),
            P("head", None),
            P(),
            P(("bend", "blk", "head"), None),
            P(("bend", "blk", "head")),
        ),
        out_specs=P(("bend", "blk", "head"), None),
        check_vma=False,
    )
```

```python
import functools

import jax
import jax.numpy as jnp
from jax import lax
from jax.experimental import pallas as pl
from jax.experimental.pallas import tpu as pltpu
from jax.sharding import PartitionSpec as P

HEADS = 12
HD = 64
LIST = 4
REACH = 3
MESH = pl.DeviceIdType.MESH


def ring_shift(block, axis, size, distance):
    route = [(i, (i + distance) % size) for i in range(size)]
    return lax.ppermute(block, axis, route)


def x_shift(block, blk_size, x_size, distance):
    route = []
    for i in range(blk_size):
        hi, x = divmod(i, x_size)
        route.append((i, hi * x_size + (x + distance) % x_size))
    return lax.ppermute(block, "blk", route)


def core_swap(block, bend_size):
    route = [(i, i ^ 1) for i in range(bend_size)]
    return lax.ppermute(block, "bend", route)


def attention_kernel(n_blocks, mask_ref, q_ref, *refs):
    kv_refs = refs[:n_blocks]
    o_ref = refs[n_blocks]
    m_scr, l_scr, acc_scr = refs[n_blocks + 1:]
    scale = 1.0 / HD**0.5
    q_t = q_ref[...].T
    first = lax.broadcasted_iota(jnp.int32, q_t.shape, 0) < HD
    zero = jnp.zeros_like(q_t)
    halves = (jnp.where(first, q_t, zero), jnp.where(first, zero, q_t))
    for hh in range(2):
        m_scr[hh] = jnp.full(m_scr.shape[1:], -jnp.inf, jnp.float32)
        l_scr[hh] = jnp.zeros(l_scr.shape[1:], jnp.float32)
        acc_scr[hh] = jnp.zeros(acc_scr.shape[1:], jnp.float32)
    for j in range(n_blocks):
        @pl.when(mask_ref[j] > 0)
        def _():
            k = kv_refs[j][0]
            for hh in range(2):
                s_t = jnp.dot(k, halves[hh], preferred_element_type=jnp.float32) * scale
                m_scr[hh] = jnp.maximum(m_scr[hh], jnp.max(s_t, axis=0, keepdims=True))
    for j in range(n_blocks):
        @pl.when(mask_ref[j] > 0)
        def _():
            k = kv_refs[j][0]
            v_t = kv_refs[j][1].T
            for hh in range(2):
                s_t = jnp.dot(k, halves[hh], preferred_element_type=jnp.float32) * scale
                w_t = jnp.exp(s_t - m_scr[hh])
                l_scr[hh] += jnp.sum(w_t, axis=0, keepdims=True)
                acc_scr[hh] += jnp.dot(v_t, w_t.astype(jnp.bfloat16),
                                       preferred_element_type=jnp.float32)
    lane = lax.broadcasted_iota(jnp.int32, acc_scr.shape[1:], 0) < HD
    out_t = jnp.where(lane, acc_scr[0] / l_scr[0], acc_scr[1] / l_scr[1])
    o_ref[...] = out_t.T.astype(o_ref.dtype)


def attend(mask, q, blocks):
    rows, width = q.shape
    n_blocks = len(blocks)
    pair = 2 * HD
    grid_spec = pltpu.PrefetchScalarGridSpec(
        num_scalar_prefetch=1,
        grid=(width // pair,),
        in_specs=[pl.BlockSpec((rows, pair), lambda p, m: (0, p))]
        + [pl.BlockSpec((2, rows, pair), lambda p, m: (0, 0, p))] * n_blocks,
        out_specs=pl.BlockSpec((rows, pair), lambda p, m: (0, p)),
        scratch_shapes=[
            pltpu.VMEM((2, 1, rows), jnp.float32),
            pltpu.VMEM((2, 1, rows), jnp.float32),
            pltpu.VMEM((2, pair, rows), jnp.float32),
        ],
    )
    return pl.pallas_call(
        functools.partial(attention_kernel, n_blocks),
        grid_spec=grid_spec,
        out_shape=jax.ShapeDtypeStruct((rows, width), jnp.bfloat16),
        cost_estimate=pl.CostEstimate(
            flops=12 * rows * rows * width * 4,
            transcendentals=rows * rows * HEADS * 4,
            bytes_accessed=2 * rows * width * (2 * n_blocks + 2),
        ),
    )(mask, q, *blocks)


def spread_kernel(x_size, up_z, down_z, out_z, up_full, down_full, out_full,
                  send_sems, recv_sems, local_sems):
    blk = lax.axis_index("blk")
    head = lax.axis_index("head")
    bend = lax.axis_index("bend")
    hi, x = blk // x_size, blk % x_size
    c = bend % 2
    left = (hi * x_size + (x + x_size - 1) % x_size, head, bend)
    right = (hi * x_size + (x + 1) % x_size, head, bend)
    partner = (blk, head, bend + 1 - 2 * c)
    p_own = x * 2 + c
    p_left = ((x + x_size - 1) % x_size) * 2 + c
    p_right = ((x + 1) % x_size) * 2 + c
    p_far = ((x + 2) % x_size) * 2 + c
    width = up_z.shape[1]
    rows = up_z.shape[0]
    heads = down_z.shape[0]

    barrier = pltpu.get_barrier_semaphore()
    for dev in (left, right, partner):
        pl.semaphore_signal(barrier, inc=1, device_id=dev, device_id_type=MESH)
    pl.semaphore_wait(barrier, 3)

    def up_at(p, part=None):
        cols = pl.ds(pl.multiple_of(p * width, 128), width)
        if part is None:
            return up_full.at[:, cols]
        return up_full.at[pl.ds(part * (rows // 2), rows // 2), cols]

    def down_at(p, part=None):
        if part is None:
            return down_full.at[:, p]
        return down_full.at[pl.ds(part * (heads // 2), heads // 2), p]

    def send(src, dst, k, dev):
        copy = pltpu.make_async_remote_copy(
            src_ref=src, dst_ref=dst, send_sem=send_sems.at[k], recv_sem=recv_sems.at[k],
            device_id=dev, device_id_type=MESH)
        copy.start()
        return copy

    local = [
        pltpu.make_async_copy(up_z, up_at(p_own), local_sems.at[0]),
        pltpu.make_async_copy(down_z, down_at(p_own), local_sems.at[1]),
        pltpu.make_async_copy(out_z, out_full.at[:, c], local_sems.at[2]),
    ]
    for copy in local:
        copy.start()
    a_up_r = send(up_z, up_at(p_own), 0, right)
    a_up_l = send(up_z, up_at(p_own), 1, left)
    a_dn_r = send(down_z, down_at(p_own), 2, right)
    a_dn_l = send(down_z, down_at(p_own), 3, left)
    sent = [a_up_r, a_up_l, a_dn_r, a_dn_l]
    sent += [
        send(out_z, out_full.at[:, c], 4, partner),
        send(up_z, up_at(p_own), 5, partner),
        send(down_z, down_at(p_own), 6, partner),
    ]
    a_up_r.wait_recv()
    a_dn_r.wait_recv()
    b_up_r = send(up_at(p_left, 0), up_at(p_left, 0), 7, right)
    b_dn_r = send(down_at(p_left, 0), down_at(p_left, 0), 8, right)
    sent += [b_up_r, b_dn_r]
    sent += [send(up_at(p_left), up_at(p_left), 9, partner),
             send(down_at(p_left), down_at(p_left), 10, partner)]
    a_up_l.wait_recv()
    a_dn_l.wait_recv()
    b_up_l = send(up_at(p_right, 1), up_at(p_right, 1), 11, left)
    b_dn_l = send(down_at(p_right, 1), down_at(p_right, 1), 12, left)
    sent += [b_up_l, b_dn_l]
    sent += [send(up_at(p_right), up_at(p_right), 13, partner),
             send(down_at(p_right), down_at(p_right), 14, partner)]
    b_up_r.wait_recv()
    b_dn_r.wait_recv()
    sent += [send(up_at(p_far, 0), up_at(p_far, 0), 15, partner),
             send(down_at(p_far, 0), down_at(p_far, 0), 16, partner)]
    b_up_l.wait_recv()
    b_dn_l.wait_recv()
    sent += [send(up_at(p_far, 1), up_at(p_far, 1), 17, partner),
             send(down_at(p_far, 1), down_at(p_far, 1), 18, partner)]
    for k in (4, 5, 6, 9, 10, 13, 14, 15, 16, 17, 18):
        sent[k].wait_recv()
    for copy in sent:
        copy.wait_send()
    for copy in local:
        copy.wait()


def spread_weights(up_z, down_z, out_z, x_size):
    rows, width = up_z.shape
    heads, down_rows, d = down_z.shape
    n_pieces = 2 * x_size
    any_spec = pl.BlockSpec(memory_space=pl.ANY)
    return pl.pallas_call(
        functools.partial(spread_kernel, x_size),
        out_shape=(
            jax.ShapeDtypeStruct((rows, n_pieces * width), up_z.dtype),
            jax.ShapeDtypeStruct((heads, n_pieces, down_rows, d), down_z.dtype),
            jax.ShapeDtypeStruct((heads, 2) + out_z.shape[1:], out_z.dtype),
        ),
        in_specs=[any_spec] * 3,
        out_specs=(any_spec, any_spec, any_spec),
        scratch_shapes=[
            pltpu.SemaphoreType.DMA((19,)),
            pltpu.SemaphoreType.DMA((19,)),
            pltpu.SemaphoreType.DMA((3,)),
        ],
        compiler_params=pltpu.CompilerParams(collective_id=1, has_side_effects=True),
    )(up_z, down_z, out_z)


def shards(
    queries,
    keys_values,
    surface,
    out_weight,
    up_weight,
    down_weight,
    norm_gain,
    block_lists,
    list_lengths,
):
    row_count, feature_width = queries.shape
    loop_size = lax.axis_size(("blk", "head"))
    blk_size = lax.axis_size("blk")
    bend_size = lax.axis_size("bend")
    x_size = 4
    own_index = lax.axis_index(("blk", "head"))
    x = lax.axis_index("blk") % x_size
    core = lax.axis_index("bend") % 2
    piece = x * 2 + core
    n_pieces = 2 * x_size

    out_rows = out_weight.shape[0] // 2
    down_rows = down_weight.shape[0] // n_pieces
    up_cols = up_weight.shape[1] // n_pieces
    pieces = (
        lax.dynamic_slice_in_dim(out_weight, core * out_rows, out_rows, axis=0),
        lax.dynamic_slice_in_dim(up_weight, piece * up_cols, up_cols, axis=1),
        lax.dynamic_slice_in_dim(down_weight, piece * down_rows, down_rows, axis=0),
    )
    sizes = [w.size for w in pieces]
    packed = jnp.concatenate([w.reshape(-1) for w in pieces])
    by_head = lax.all_gather(packed, "head", axis=0, tiled=False)
    n_heads = by_head.shape[0]
    d = feature_width
    o0, o1 = sizes[0], sizes[0] + sizes[1]
    out_z = by_head[:, :o0].reshape(n_heads, out_rows, d)
    up_z = by_head[:, o0:o1].reshape(-1, up_cols)
    down_z = by_head[:, o1:].reshape(n_heads, down_rows, d)
    up_full, down_full, out_full = spread_weights(up_z, down_z, out_z, x_size)
    out_full = out_full.reshape(d, d)
    down_full = down_full.reshape(-1, d)

    blocks = [keys_values]
    ids = [own_index]
    left = right = keys_values
    for d in range(1, REACH + 1):
        left = ring_shift(left, ("blk", "head"), loop_size, 1)
        right = ring_shift(right, ("blk", "head"), loop_size, -1)
        blocks += [left, right]
        ids += [(own_index - d) % loop_size, (own_index + d) % loop_size]
    entry_live = jnp.arange(LIST, dtype=jnp.int32) < list_lengths[0]
    mask = jnp.stack(
        [jnp.any((block_lists[0] == b) & entry_live) for b in ids]).astype(jnp.int32)
    context = attend(mask, queries, blocks)

    hidden = surface.astype(jnp.float32) + jnp.dot(
        context, out_full, preferred_element_type=jnp.float32)
    mean_square = jnp.mean(hidden * hidden, axis=1, keepdims=True)
    normed = (hidden * lax.rsqrt(mean_square + 1e-05) * norm_gain[None, :]).astype(jnp.bfloat16)
    pre_gelu = jnp.dot(normed, up_full, preferred_element_type=jnp.float32)
    activated = jax.nn.gelu(pre_gelu, approximate=True).astype(jnp.bfloat16)
    mixed_out = hidden + jnp.dot(activated, down_full, preferred_element_type=jnp.float32)
    return mixed_out.astype(jnp.bfloat16)


def solution(mesh):
    return jax.shard_map(
        shards,
        mesh=mesh,
        in_specs=(
            P(("bend", "blk", "head"), None),
            P(None, ("bend", "blk", "head"), None),
            P(("bend", "blk", "head"), None),
            P("head", None),
            P("head", None),
            P("head", None),
            P(),
            P(("bend", "blk", "head"), None),
            P(("bend", "blk", "head")),
        ),
        out_specs=P(("bend", "blk", "head"), None),
        check_vma=False,
    )
```

```python
import functools

import jax
import jax.numpy as jnp
from jax import lax
from jax.experimental import pallas as pl
from jax.experimental.pallas import tpu as pltpu
from jax.sharding import PartitionSpec as P

HEADS = 12
HD = 64
LIST = 4
REACH = 3
MESH = pl.DeviceIdType.MESH


def ring_shift(block, axis, size, distance):
    route = [(i, (i + distance) % size) for i in range(size)]
    return lax.ppermute(block, axis, route)


def x_shift(block, blk_size, x_size, distance):
    route = []
    for i in range(blk_size):
        hi, x = divmod(i, x_size)
        route.append((i, hi * x_size + (x + distance) % x_size))
    return lax.ppermute(block, "blk", route)


def core_swap(block, bend_size):
    route = [(i, i ^ 1) for i in range(bend_size)]
    return lax.ppermute(block, "bend", route)


def attention_kernel(n_blocks, mask_ref, q_ref, *refs):
    kv_refs = refs[:n_blocks]
    o_ref = refs[n_blocks]
    m_scr, l_scr, acc_scr = refs[n_blocks + 1:]
    scale = 1.0 / HD**0.5
    q_t = q_ref[...].T
    first = lax.broadcasted_iota(jnp.int32, q_t.shape, 0) < HD
    zero = jnp.zeros_like(q_t)
    halves = (jnp.where(first, q_t, zero), jnp.where(first, zero, q_t))
    for hh in range(2):
        m_scr[hh] = jnp.full(m_scr.shape[1:], -jnp.inf, jnp.float32)
        l_scr[hh] = jnp.zeros(l_scr.shape[1:], jnp.float32)
        acc_scr[hh] = jnp.zeros(acc_scr.shape[1:], jnp.float32)
    for j in range(n_blocks):
        @pl.when(mask_ref[j] > 0)
        def _():
            k = kv_refs[j][0]
            for hh in range(2):
                s_t = jnp.dot(k, halves[hh], preferred_element_type=jnp.float32) * scale
                m_scr[hh] = jnp.maximum(m_scr[hh], jnp.max(s_t, axis=0, keepdims=True))
    for j in range(n_blocks):
        @pl.when(mask_ref[j] > 0)
        def _():
            k = kv_refs[j][0]
            v_t = kv_refs[j][1].T
            for hh in range(2):
                s_t = jnp.dot(k, halves[hh], preferred_element_type=jnp.float32) * scale
                w_t = jnp.exp(s_t - m_scr[hh])
                l_scr[hh] += jnp.sum(w_t, axis=0, keepdims=True)
                acc_scr[hh] += jnp.dot(v_t, w_t.astype(jnp.bfloat16),
                                       preferred_element_type=jnp.float32)
    lane = lax.broadcasted_iota(jnp.int32, acc_scr.shape[1:], 0) < HD
    out_t = jnp.where(lane, acc_scr[0] / l_scr[0], acc_scr[1] / l_scr[1])
    o_ref[...] = out_t.T.astype(o_ref.dtype)


def attend(mask, q, blocks):
    rows, width = q.shape
    n_blocks = len(blocks)
    pair = 2 * HD
    grid_spec = pltpu.PrefetchScalarGridSpec(
        num_scalar_prefetch=1,
        grid=(width // pair,),
        in_specs=[pl.BlockSpec((rows, pair), lambda p, m: (0, p))]
        + [pl.BlockSpec((2, rows, pair), lambda p, m: (0, 0, p))] * n_blocks,
        out_specs=pl.BlockSpec((rows, pair), lambda p, m: (0, p)),
        scratch_shapes=[
            pltpu.VMEM((2, 1, rows), jnp.float32),
            pltpu.VMEM((2, 1, rows), jnp.float32),
            pltpu.VMEM((2, pair, rows), jnp.float32),
        ],
    )
    return pl.pallas_call(
        functools.partial(attention_kernel, n_blocks),
        grid_spec=grid_spec,
        out_shape=jax.ShapeDtypeStruct((rows, width), jnp.bfloat16),
        cost_estimate=pl.CostEstimate(
            flops=12 * rows * rows * width * 4,
            transcendentals=rows * rows * HEADS * 4,
            bytes_accessed=2 * rows * width * (2 * n_blocks + 2),
        ),
    )(mask, q, *blocks)


def spread_kernel(x_size, kv, up_z, down_z, out_z, kv_out, up_full, down_full, out_full,
                  send_sems, recv_sems, local_sems, kv_send, kv_recv):
    blk = lax.axis_index("blk")
    head = lax.axis_index("head")
    bend = lax.axis_index("bend")
    hi, x = blk // x_size, blk % x_size
    c = bend % 2
    left = (hi * x_size + (x + x_size - 1) % x_size, head, bend)
    right = (hi * x_size + (x + 1) % x_size, head, bend)
    partner = (blk, head, bend + 1 - 2 * c)
    n_head = lax.axis_size("head")
    n_ring = lax.axis_size("blk") * n_head
    me = blk * n_head + head
    ring_right = ((me + 1) % n_ring // n_head, (me + 1) % n_head, bend)
    ring_left = ((me + n_ring - 1) % n_ring // n_head, (me + n_ring - 1) % n_head, bend)
    p_own = x * 2 + c
    p_left = ((x + x_size - 1) % x_size) * 2 + c
    p_right = ((x + 1) % x_size) * 2 + c
    p_far = ((x + 2) % x_size) * 2 + c
    width = up_z.shape[1]
    rows = up_z.shape[0]
    heads = down_z.shape[0]

    barrier = pltpu.get_barrier_semaphore()
    for dev in (left, right, partner, ring_left, ring_right):
        pl.semaphore_signal(barrier, inc=1, device_id=dev, device_id_type=MESH)
    pl.semaphore_wait(barrier, 5)

    def kv_send_to(src, slot, dev):
        copy = pltpu.make_async_remote_copy(
            src_ref=src, dst_ref=kv_out.at[slot], send_sem=kv_send.at[slot],
            recv_sem=kv_recv.at[slot], device_id=dev, device_id_type=MESH)
        copy.start()
        return copy

    kv_sent = [kv_send_to(kv, 0, ring_right), kv_send_to(kv, 1, ring_left)]

    def up_at(p, part=None):
        cols = pl.ds(pl.multiple_of(p * width, 128), width)
        if part is None:
            return up_full.at[:, cols]
        return up_full.at[pl.ds(part * (rows // 2), rows // 2), cols]

    def down_at(p, part=None):
        if part is None:
            return down_full.at[:, p]
        return down_full.at[pl.ds(part * (heads // 2), heads // 2), p]

    def send(src, dst, k, dev):
        copy = pltpu.make_async_remote_copy(
            src_ref=src, dst_ref=dst, send_sem=send_sems.at[k], recv_sem=recv_sems.at[k],
            device_id=dev, device_id_type=MESH)
        copy.start()
        return copy

    local = [
        pltpu.make_async_copy(up_z, up_at(p_own), local_sems.at[0]),
        pltpu.make_async_copy(down_z, down_at(p_own), local_sems.at[1]),
        pltpu.make_async_copy(out_z, out_full.at[:, c], local_sems.at[2]),
    ]
    for copy in local:
        copy.start()
    a_up_r = send(up_z, up_at(p_own), 0, right)
    a_up_l = send(up_z, up_at(p_own), 1, left)
    a_dn_r = send(down_z, down_at(p_own), 2, right)
    a_dn_l = send(down_z, down_at(p_own), 3, left)
    sent = [a_up_r, a_up_l, a_dn_r, a_dn_l]
    sent += [
        send(out_z, out_full.at[:, c], 4, partner),
        send(up_z, up_at(p_own), 5, partner),
        send(down_z, down_at(p_own), 6, partner),
    ]
    kv_sent[0].wait_recv()
    kv_sent[1].wait_recv()
    kv_sent += [kv_send_to(kv_out.at[0], 2, ring_right), kv_send_to(kv_out.at[1], 3, ring_left)]
    a_up_r.wait_recv()
    a_dn_r.wait_recv()
    b_up_r = send(up_at(p_left, 0), up_at(p_left, 0), 7, right)
    b_dn_r = send(down_at(p_left, 0), down_at(p_left, 0), 8, right)
    sent += [b_up_r, b_dn_r]
    sent += [send(up_at(p_left), up_at(p_left), 9, partner),
             send(down_at(p_left), down_at(p_left), 10, partner)]
    a_up_l.wait_recv()
    a_dn_l.wait_recv()
    b_up_l = send(up_at(p_right, 1), up_at(p_right, 1), 11, left)
    b_dn_l = send(down_at(p_right, 1), down_at(p_right, 1), 12, left)
    sent += [b_up_l, b_dn_l]
    sent += [send(up_at(p_right), up_at(p_right), 13, partner),
             send(down_at(p_right), down_at(p_right), 14, partner)]
    kv_sent[2].wait_recv()
    kv_sent[3].wait_recv()
    kv_sent += [kv_send_to(kv_out.at[2], 4, ring_right), kv_send_to(kv_out.at[3], 5, ring_left)]
    b_up_r.wait_recv()
    b_dn_r.wait_recv()
    sent += [send(up_at(p_far, 0), up_at(p_far, 0), 15, partner),
             send(down_at(p_far, 0), down_at(p_far, 0), 16, partner)]
    b_up_l.wait_recv()
    b_dn_l.wait_recv()
    sent += [send(up_at(p_far, 1), up_at(p_far, 1), 17, partner),
             send(down_at(p_far, 1), down_at(p_far, 1), 18, partner)]
    for k in (4, 5, 6, 9, 10, 13, 14, 15, 16, 17, 18):
        sent[k].wait_recv()
    kv_sent[4].wait_recv()
    kv_sent[5].wait_recv()
    for copy in sent + kv_sent:
        copy.wait_send()
    for copy in local:
        copy.wait()


def exchange(kv, up_z, down_z, out_z, x_size):
    rows, width = up_z.shape
    heads, down_rows, d = down_z.shape
    n_pieces = 2 * x_size
    any_spec = pl.BlockSpec(memory_space=pl.ANY)
    return pl.pallas_call(
        functools.partial(spread_kernel, x_size),
        out_shape=(
            jax.ShapeDtypeStruct((2 * REACH,) + kv.shape, kv.dtype),
            jax.ShapeDtypeStruct((rows, n_pieces * width), up_z.dtype),
            jax.ShapeDtypeStruct((heads, n_pieces, down_rows, d), down_z.dtype),
            jax.ShapeDtypeStruct((heads, 2) + out_z.shape[1:], out_z.dtype),
        ),
        in_specs=[any_spec] * 4,
        out_specs=(any_spec, any_spec, any_spec, any_spec),
        scratch_shapes=[
            pltpu.SemaphoreType.DMA((19,)),
            pltpu.SemaphoreType.DMA((19,)),
            pltpu.SemaphoreType.DMA((3,)),
            pltpu.SemaphoreType.DMA((2 * REACH,)),
            pltpu.SemaphoreType.DMA((2 * REACH,)),
        ],
        compiler_params=pltpu.CompilerParams(collective_id=1, has_side_effects=True),
    )(kv, up_z, down_z, out_z)


def shards(
    queries,
    keys_values,
    surface,
    out_weight,
    up_weight,
    down_weight,
    norm_gain,
    block_lists,
    list_lengths,
):
    row_count, feature_width = queries.shape
    loop_size = lax.axis_size(("blk", "head"))
    blk_size = lax.axis_size("blk")
    bend_size = lax.axis_size("bend")
    x_size = 4
    own_index = lax.axis_index(("blk", "head"))
    x = lax.axis_index("blk") % x_size
    core = lax.axis_index("bend") % 2
    piece = x * 2 + core
    n_pieces = 2 * x_size

    out_rows = out_weight.shape[0] // 2
    down_rows = down_weight.shape[0] // n_pieces
    up_cols = up_weight.shape[1] // n_pieces
    pieces = (
        lax.dynamic_slice_in_dim(out_weight, core * out_rows, out_rows, axis=0),
        lax.dynamic_slice_in_dim(up_weight, piece * up_cols, up_cols, axis=1),
        lax.dynamic_slice_in_dim(down_weight, piece * down_rows, down_rows, axis=0),
    )
    sizes = [w.size for w in pieces]
    packed = jnp.concatenate([w.reshape(-1) for w in pieces])
    by_head = lax.all_gather(packed, "head", axis=0, tiled=False)
    n_heads = by_head.shape[0]
    d = feature_width
    o0, o1 = sizes[0], sizes[0] + sizes[1]
    out_z = by_head[:, :o0].reshape(n_heads, out_rows, d)
    up_z = by_head[:, o0:o1].reshape(-1, up_cols)
    down_z = by_head[:, o1:].reshape(n_heads, down_rows, d)
    near, up_full, down_full, out_full = exchange(keys_values, up_z, down_z, out_z, x_size)
    out_full = out_full.reshape(d, d)
    down_full = down_full.reshape(-1, d)

    blocks = [keys_values]
    ids = [own_index]
    for dist in range(1, REACH + 1):
        blocks += [near[2 * dist - 2], near[2 * dist - 1]]
        ids += [(own_index - dist) % loop_size, (own_index + dist) % loop_size]
    entry_live = jnp.arange(LIST, dtype=jnp.int32) < list_lengths[0]
    mask = jnp.stack(
        [jnp.any((block_lists[0] == b) & entry_live) for b in ids]).astype(jnp.int32)
    context = attend(mask, queries, blocks)

    hidden = surface.astype(jnp.float32) + jnp.dot(
        context, out_full, preferred_element_type=jnp.float32)
    mean_square = jnp.mean(hidden * hidden, axis=1, keepdims=True)
    normed = (hidden * lax.rsqrt(mean_square + 1e-05) * norm_gain[None, :]).astype(jnp.bfloat16)
    pre_gelu = jnp.dot(normed, up_full, preferred_element_type=jnp.float32)
    activated = jax.nn.gelu(pre_gelu, approximate=True).astype(jnp.bfloat16)
    mixed_out = hidden + jnp.dot(activated, down_full, preferred_element_type=jnp.float32)
    return mixed_out.astype(jnp.bfloat16)


def solution(mesh):
    return jax.shard_map(
        shards,
        mesh=mesh,
        in_specs=(
            P(("bend", "blk", "head"), None),
            P(None, ("bend", "blk", "head"), None),
            P(("bend", "blk", "head"), None),
            P("head", None),
            P("head", None),
            P("head", None),
            P(),
            P(("bend", "blk", "head"), None),
            P(("bend", "blk", "head")),
        ),
        out_specs=P(("bend", "blk", "head"), None),
        check_vma=False,
    )
```

```python
import functools

import jax
import jax.numpy as jnp
from jax import lax
from jax.experimental import pallas as pl
from jax.experimental.pallas import tpu as pltpu
from jax.sharding import PartitionSpec as P

HEADS = 12
HD = 64
LIST = 4
REACH = 3
MESH = pl.DeviceIdType.MESH


def ring_shift(block, axis, size, distance):
    route = [(i, (i + distance) % size) for i in range(size)]
    return lax.ppermute(block, axis, route)


def x_shift(block, blk_size, x_size, distance):
    route = []
    for i in range(blk_size):
        hi, x = divmod(i, x_size)
        route.append((i, hi * x_size + (x + distance) % x_size))
    return lax.ppermute(block, "blk", route)


def core_swap(block, bend_size):
    route = [(i, i ^ 1) for i in range(bend_size)]
    return lax.ppermute(block, "bend", route)


def attention_kernel(n_blocks, mask_ref, q_ref, *refs):
    kv_refs = refs[:n_blocks]
    o_ref = refs[n_blocks]
    m_scr, l_scr, acc_scr = refs[n_blocks + 1:]
    scale = 1.0 / HD**0.5
    q_t = q_ref[...].T
    first = lax.broadcasted_iota(jnp.int32, q_t.shape, 0) < HD
    zero = jnp.zeros_like(q_t)
    halves = (jnp.where(first, q_t, zero), jnp.where(first, zero, q_t))
    for hh in range(2):
        m_scr[hh] = jnp.full(m_scr.shape[1:], -jnp.inf, jnp.float32)
        l_scr[hh] = jnp.zeros(l_scr.shape[1:], jnp.float32)
        acc_scr[hh] = jnp.zeros(acc_scr.shape[1:], jnp.float32)
    for j in range(n_blocks):
        @pl.when(mask_ref[j] > 0)
        def _():
            k = kv_refs[j][0]
            for hh in range(2):
                s_t = jnp.dot(k, halves[hh], preferred_element_type=jnp.float32) * scale
                m_scr[hh] = jnp.maximum(m_scr[hh], jnp.max(s_t, axis=0, keepdims=True))
    for j in range(n_blocks):
        @pl.when(mask_ref[j] > 0)
        def _():
            k = kv_refs[j][0]
            v_t = kv_refs[j][1].T
            for hh in range(2):
                s_t = jnp.dot(k, halves[hh], preferred_element_type=jnp.float32) * scale
                w_t = jnp.exp(s_t - m_scr[hh])
                l_scr[hh] += jnp.sum(w_t, axis=0, keepdims=True)
                acc_scr[hh] += jnp.dot(v_t, w_t.astype(jnp.bfloat16),
                                       preferred_element_type=jnp.float32)
    lane = lax.broadcasted_iota(jnp.int32, acc_scr.shape[1:], 0) < HD
    out_t = jnp.where(lane, acc_scr[0] / l_scr[0], acc_scr[1] / l_scr[1])
    o_ref[...] = out_t.T.astype(o_ref.dtype)


def attend(mask, q, blocks):
    rows, width = q.shape
    n_blocks = len(blocks)
    pair = 2 * HD
    grid_spec = pltpu.PrefetchScalarGridSpec(
        num_scalar_prefetch=1,
        grid=(width // pair,),
        in_specs=[pl.BlockSpec((rows, pair), lambda p, m: (0, p))]
        + [pl.BlockSpec((2, rows, pair), lambda p, m: (0, 0, p))] * n_blocks,
        out_specs=pl.BlockSpec((rows, pair), lambda p, m: (0, p)),
        scratch_shapes=[
            pltpu.VMEM((2, 1, rows), jnp.float32),
            pltpu.VMEM((2, 1, rows), jnp.float32),
            pltpu.VMEM((2, pair, rows), jnp.float32),
        ],
    )
    return pl.pallas_call(
        functools.partial(attention_kernel, n_blocks),
        grid_spec=grid_spec,
        out_shape=jax.ShapeDtypeStruct((rows, width), jnp.bfloat16),
        cost_estimate=pl.CostEstimate(
            flops=12 * rows * rows * width * 4,
            transcendentals=rows * rows * HEADS * 4,
            bytes_accessed=2 * rows * width * (2 * n_blocks + 2),
        ),
    )(mask, q, *blocks)


def spread_kernel(x_size, bias_ref, q_ref, kv, up_z, down_z, out_z,
                  ctx_ref, up_full, down_full, out_full,
                  slots, q_t, m_scr, l_scr, acc_scr,
                  send_sems, recv_sems, local_sems, kv_send, kv_recv):
    blk = lax.axis_index("blk")
    head = lax.axis_index("head")
    bend = lax.axis_index("bend")
    hi, x = blk // x_size, blk % x_size
    c = bend % 2
    left = (hi * x_size + (x + x_size - 1) % x_size, head, bend)
    right = (hi * x_size + (x + 1) % x_size, head, bend)
    partner = (blk, head, bend + 1 - 2 * c)
    n_head = lax.axis_size("head")
    n_ring = lax.axis_size("blk") * n_head
    me = blk * n_head + head
    ring_right = ((me + 1) % n_ring // n_head, (me + 1) % n_head, bend)
    ring_left = ((me + n_ring - 1) % n_ring // n_head, (me + n_ring - 1) % n_head, bend)
    p_own = x * 2 + c
    p_left = ((x + x_size - 1) % x_size) * 2 + c
    p_right = ((x + 1) % x_size) * 2 + c
    p_far = ((x + 2) % x_size) * 2 + c
    width = up_z.shape[1]
    rows = up_z.shape[0]
    heads = down_z.shape[0]
    pair = 2 * HD
    n_pairs = q_ref.shape[1] // pair
    scale = 1.0 / HD**0.5

    barrier = pltpu.get_barrier_semaphore()
    for dev in (left, right, partner, ring_left, ring_right):
        pl.semaphore_signal(barrier, inc=1, device_id=dev, device_id_type=MESH)
    pl.semaphore_wait(barrier, 5)

    def kv_send_to(src, slot, dev):
        copy = pltpu.make_async_remote_copy(
            src_ref=src, dst_ref=slots.at[slot], send_sem=kv_send.at[slot],
            recv_sem=kv_recv.at[slot], device_id=dev, device_id_type=MESH)
        copy.start()
        return copy

    def up_at(p, part=None):
        cols = pl.ds(pl.multiple_of(p * width, 128), width)
        if part is None:
            return up_full.at[:, cols]
        return up_full.at[pl.ds(part * (rows // 2), rows // 2), cols]

    def down_at(p, part=None):
        if part is None:
            return down_full.at[:, p]
        return down_full.at[pl.ds(part * (heads // 2), heads // 2), p]

    def send(src, dst, k, dev):
        copy = pltpu.make_async_remote_copy(
            src_ref=src, dst_ref=dst, send_sem=send_sems.at[k], recv_sem=recv_sems.at[k],
            device_id=dev, device_id_type=MESH)
        copy.start()
        return copy

    kv_sent = [kv_send_to(kv, 0, ring_right), kv_send_to(kv, 1, ring_left)]
    local = [
        pltpu.make_async_copy(up_z, up_at(p_own), local_sems.at[0]),
        pltpu.make_async_copy(down_z, down_at(p_own), local_sems.at[1]),
        pltpu.make_async_copy(out_z, out_full.at[:, c], local_sems.at[2]),
    ]
    for copy in local:
        copy.start()
    a_up_r = send(up_z, up_at(p_own), 0, right)
    a_up_l = send(up_z, up_at(p_own), 1, left)
    a_dn_r = send(down_z, down_at(p_own), 2, right)
    a_dn_l = send(down_z, down_at(p_own), 3, left)
    sent = [a_up_r, a_up_l, a_dn_r, a_dn_l]
    sent += [
        send(out_z, out_full.at[:, c], 4, partner),
        send(up_z, up_at(p_own), 5, partner),
        send(down_z, down_at(p_own), 6, partner),
    ]

    first = lax.broadcasted_iota(jnp.int32, (pair, q_ref.shape[0]), 0) < HD
    for p in range(n_pairs):
        qp = q_ref[:, p * pair:(p + 1) * pair].T
        q_t[2 * p] = jnp.where(first, qp, jnp.zeros_like(qp))
        q_t[2 * p + 1] = jnp.where(first, jnp.zeros_like(qp), qp)
    m_scr[...] = jnp.full(m_scr.shape, -jnp.inf, jnp.float32)
    l_scr[...] = jnp.zeros(l_scr.shape, jnp.float32)
    acc_scr[...] = jnp.zeros(acc_scr.shape, jnp.float32)

    def absorb(block, bias):
        def one_pair(p, carry):
            cols = pl.ds(pl.multiple_of(p * pair, pair), pair)
            k = block[0, :, cols]
            v_t = block[1, :, cols].T
            for hh in range(2):
                h = 2 * p + hh
                s_t = jnp.dot(k, q_t[h], preferred_element_type=jnp.float32) * scale + bias
                m_old = m_scr[h]
                m_new = jnp.maximum(m_old, jnp.max(s_t, axis=0, keepdims=True))
                alpha = jnp.exp(m_old - m_new)
                w_t = jnp.exp(s_t - m_new)
                l_scr[h] = alpha * l_scr[h] + jnp.sum(w_t, axis=0, keepdims=True)
                acc_scr[h] = alpha * acc_scr[h] + jnp.dot(
                    v_t, w_t.astype(jnp.bfloat16), preferred_element_type=jnp.float32)
                m_scr[h] = m_new
            return carry
        lax.fori_loop(0, n_pairs, one_pair, 0)

    absorb(kv, bias_ref[0])

    kv_sent[0].wait_recv()
    kv_sent[1].wait_recv()
    kv_sent += [kv_send_to(slots.at[0], 2, ring_right), kv_send_to(slots.at[1], 3, ring_left)]
    a_up_r.wait_recv()
    a_dn_r.wait_recv()
    b_up_r = send(up_at(p_left, 0), up_at(p_left, 0), 7, right)
    b_dn_r = send(down_at(p_left, 0), down_at(p_left, 0), 8, right)
    sent += [b_up_r, b_dn_r]
    sent += [send(up_at(p_left), up_at(p_left), 9, partner),
             send(down_at(p_left), down_at(p_left), 10, partner)]
    a_up_l.wait_recv()
    a_dn_l.wait_recv()
    b_up_l = send(up_at(p_right, 1), up_at(p_right, 1), 11, left)
    b_dn_l = send(down_at(p_right, 1), down_at(p_right, 1), 12, left)
    sent += [b_up_l, b_dn_l]
    sent += [send(up_at(p_right), up_at(p_right), 13, partner),
             send(down_at(p_right), down_at(p_right), 14, partner)]

    absorb(slots.at[0], bias_ref[1])
    absorb(slots.at[1], bias_ref[2])

    kv_sent[2].wait_recv()
    kv_sent[3].wait_recv()
    kv_sent += [kv_send_to(slots.at[2], 4, ring_right), kv_send_to(slots.at[3], 5, ring_left)]
    b_up_r.wait_recv()
    b_dn_r.wait_recv()
    sent += [send(up_at(p_far, 0), up_at(p_far, 0), 15, partner),
             send(down_at(p_far, 0), down_at(p_far, 0), 16, partner)]
    b_up_l.wait_recv()
    b_dn_l.wait_recv()
    sent += [send(up_at(p_far, 1), up_at(p_far, 1), 17, partner),
             send(down_at(p_far, 1), down_at(p_far, 1), 18, partner)]

    absorb(slots.at[2], bias_ref[3])
    absorb(slots.at[3], bias_ref[4])

    kv_sent[4].wait_recv()
    kv_sent[5].wait_recv()
    absorb(slots.at[4], bias_ref[5])
    absorb(slots.at[5], bias_ref[6])

    row = lax.broadcasted_iota(jnp.int32, (pair, q_ref.shape[0]), 0) < HD

    def write_pair(p, carry):
        out_t = jnp.where(row, acc_scr[2 * p] / l_scr[2 * p], acc_scr[2 * p + 1] / l_scr[2 * p + 1])
        ctx_ref[:, pl.ds(pl.multiple_of(p * pair, pair), pair)] = out_t.T.astype(ctx_ref.dtype)
        return carry
    lax.fori_loop(0, n_pairs, write_pair, 0)

    for k in (4, 5, 6, 9, 10, 13, 14, 15, 16, 17, 18):
        sent[k].wait_recv()
    for copy in sent + kv_sent:
        copy.wait_send()
    for copy in local:
        copy.wait()


def exchange(bias, q, kv, up_z, down_z, out_z, x_size):
    rows, width = up_z.shape
    heads, down_rows, d = down_z.shape
    n_rows = q.shape[0]
    n_pieces = 2 * x_size
    any_spec = pl.BlockSpec(memory_space=pl.ANY)
    vmem_spec = pl.BlockSpec(memory_space=pltpu.VMEM)
    return pl.pallas_call(
        functools.partial(spread_kernel, x_size),
        out_shape=(
            jax.ShapeDtypeStruct(q.shape, jnp.bfloat16),
            jax.ShapeDtypeStruct((rows, n_pieces * width), up_z.dtype),
            jax.ShapeDtypeStruct((heads, n_pieces, down_rows, d), down_z.dtype),
            jax.ShapeDtypeStruct((heads, 2) + out_z.shape[1:], out_z.dtype),
        ),
        in_specs=[pl.BlockSpec(memory_space=pltpu.SMEM), vmem_spec, vmem_spec,
                  any_spec, any_spec, any_spec],
        out_specs=(vmem_spec, any_spec, any_spec, any_spec),
        scratch_shapes=[
            pltpu.VMEM((2 * REACH,) + kv.shape, kv.dtype),
            pltpu.VMEM((HEADS, 2 * HD, n_rows), jnp.bfloat16),
            pltpu.VMEM((HEADS, 1, n_rows), jnp.float32),
            pltpu.VMEM((HEADS, 1, n_rows), jnp.float32),
            pltpu.VMEM((HEADS, 2 * HD, n_rows), jnp.float32),
            pltpu.SemaphoreType.DMA((19,)),
            pltpu.SemaphoreType.DMA((19,)),
            pltpu.SemaphoreType.DMA((3,)),
            pltpu.SemaphoreType.DMA((2 * REACH,)),
            pltpu.SemaphoreType.DMA((2 * REACH,)),
        ],
        compiler_params=pltpu.CompilerParams(
            collective_id=1, has_side_effects=True, vmem_limit_bytes=48 * 1024 * 1024),
        cost_estimate=pl.CostEstimate(
            flops=6 * n_rows * n_rows * q.shape[1] * (2 * REACH + 1),
            transcendentals=n_rows * n_rows * HEADS * (2 * REACH + 1),
            bytes_accessed=2 * (rows * n_pieces * width + heads * n_pieces * down_rows * d),
        ),
    )(bias, q, kv, up_z, down_z, out_z)


def shards(
    queries,
    keys_values,
    surface,
    out_weight,
    up_weight,
    down_weight,
    norm_gain,
    block_lists,
    list_lengths,
):
    row_count, feature_width = queries.shape
    loop_size = lax.axis_size(("blk", "head"))
    blk_size = lax.axis_size("blk")
    bend_size = lax.axis_size("bend")
    x_size = 4
    own_index = lax.axis_index(("blk", "head"))
    x = lax.axis_index("blk") % x_size
    core = lax.axis_index("bend") % 2
    piece = x * 2 + core
    n_pieces = 2 * x_size

    out_rows = out_weight.shape[0] // 2
    down_rows = down_weight.shape[0] // n_pieces
    up_cols = up_weight.shape[1] // n_pieces
    pieces = (
        lax.dynamic_slice_in_dim(out_weight, core * out_rows, out_rows, axis=0),
        lax.dynamic_slice_in_dim(up_weight, piece * up_cols, up_cols, axis=1),
        lax.dynamic_slice_in_dim(down_weight, piece * down_rows, down_rows, axis=0),
    )
    sizes = [w.size for w in pieces]
    packed = jnp.concatenate([w.reshape(-1) for w in pieces])
    by_head = lax.all_gather(packed, "head", axis=0, tiled=False)
    n_heads = by_head.shape[0]
    d = feature_width
    o0, o1 = sizes[0], sizes[0] + sizes[1]
    out_z = by_head[:, :o0].reshape(n_heads, out_rows, d)
    up_z = by_head[:, o0:o1].reshape(-1, up_cols)
    down_z = by_head[:, o1:].reshape(n_heads, down_rows, d)
    ids = [own_index]
    for dist in range(1, REACH + 1):
        ids += [(own_index - dist) % loop_size, (own_index + dist) % loop_size]
    entry_live = jnp.arange(LIST, dtype=jnp.int32) < list_lengths[0]
    listed = jnp.stack([jnp.any((block_lists[0] == b) & entry_live) for b in ids])
    bias = jnp.where(listed, 0.0, -1e30).astype(jnp.float32)
    context, up_full, down_full, out_full = exchange(
        bias, queries, keys_values, up_z, down_z, out_z, x_size)
    out_full = out_full.reshape(d, d)
    down_full = down_full.reshape(-1, d)

    hidden = surface.astype(jnp.float32) + jnp.dot(
        context, out_full, preferred_element_type=jnp.float32)
    mean_square = jnp.mean(hidden * hidden, axis=1, keepdims=True)
    normed = (hidden * lax.rsqrt(mean_square + 1e-05) * norm_gain[None, :]).astype(jnp.bfloat16)
    pre_gelu = jnp.dot(normed, up_full, preferred_element_type=jnp.float32)
    activated = jax.nn.gelu(pre_gelu, approximate=True).astype(jnp.bfloat16)
    mixed_out = hidden + jnp.dot(activated, down_full, preferred_element_type=jnp.float32)
    return mixed_out.astype(jnp.bfloat16)


def solution(mesh):
    return jax.shard_map(
        shards,
        mesh=mesh,
        in_specs=(
            P(("bend", "blk", "head"), None),
            P(None, ("bend", "blk", "head"), None),
            P(("bend", "blk", "head"), None),
            P("head", None),
            P("head", None),
            P("head", None),
            P(),
            P(("bend", "blk", "head"), None),
            P(("bend", "blk", "head")),
        ),
        out_specs=P(("bend", "blk", "head"), None),
        check_vma=False,
    )
```

```python
import functools

import jax
import jax.numpy as jnp
from jax import lax
from jax.experimental import pallas as pl
from jax.experimental.pallas import tpu as pltpu
from jax.sharding import PartitionSpec as P

HEADS = 12
HD = 64
LIST = 4
REACH = 3
MESH = pl.DeviceIdType.MESH


def ring_shift(block, axis, size, distance):
    route = [(i, (i + distance) % size) for i in range(size)]
    return lax.ppermute(block, axis, route)


def x_shift(block, blk_size, x_size, distance):
    route = []
    for i in range(blk_size):
        hi, x = divmod(i, x_size)
        route.append((i, hi * x_size + (x + distance) % x_size))
    return lax.ppermute(block, "blk", route)


def core_swap(block, bend_size):
    route = [(i, i ^ 1) for i in range(bend_size)]
    return lax.ppermute(block, "bend", route)


def attention_kernel(n_blocks, mask_ref, q_ref, *refs):
    kv_refs = refs[:n_blocks]
    o_ref = refs[n_blocks]
    m_scr, l_scr, acc_scr = refs[n_blocks + 1:]
    scale = 1.0 / HD**0.5
    q_t = q_ref[...].T
    first = lax.broadcasted_iota(jnp.int32, q_t.shape, 0) < HD
    zero = jnp.zeros_like(q_t)
    halves = (jnp.where(first, q_t, zero), jnp.where(first, zero, q_t))
    for hh in range(2):
        m_scr[hh] = jnp.full(m_scr.shape[1:], -jnp.inf, jnp.float32)
        l_scr[hh] = jnp.zeros(l_scr.shape[1:], jnp.float32)
        acc_scr[hh] = jnp.zeros(acc_scr.shape[1:], jnp.float32)
    for j in range(n_blocks):
        @pl.when(mask_ref[j] > 0)
        def _():
            k = kv_refs[j][0]
            for hh in range(2):
                s_t = jnp.dot(k, halves[hh], preferred_element_type=jnp.float32) * scale
                m_scr[hh] = jnp.maximum(m_scr[hh], jnp.max(s_t, axis=0, keepdims=True))
    for j in range(n_blocks):
        @pl.when(mask_ref[j] > 0)
        def _():
            k = kv_refs[j][0]
            v_t = kv_refs[j][1].T
            for hh in range(2):
                s_t = jnp.dot(k, halves[hh], preferred_element_type=jnp.float32) * scale
                w_t = jnp.exp(s_t - m_scr[hh])
                l_scr[hh] += jnp.sum(w_t, axis=0, keepdims=True)
                acc_scr[hh] += jnp.dot(v_t, w_t.astype(jnp.bfloat16),
                                       preferred_element_type=jnp.float32)
    lane = lax.broadcasted_iota(jnp.int32, acc_scr.shape[1:], 0) < HD
    out_t = jnp.where(lane, acc_scr[0] / l_scr[0], acc_scr[1] / l_scr[1])
    o_ref[...] = out_t.T.astype(o_ref.dtype)


def attend(mask, q, blocks):
    rows, width = q.shape
    n_blocks = len(blocks)
    pair = 2 * HD
    grid_spec = pltpu.PrefetchScalarGridSpec(
        num_scalar_prefetch=1,
        grid=(width // pair,),
        in_specs=[pl.BlockSpec((rows, pair), lambda p, m: (0, p))]
        + [pl.BlockSpec((2, rows, pair), lambda p, m: (0, 0, p))] * n_blocks,
        out_specs=pl.BlockSpec((rows, pair), lambda p, m: (0, p)),
        scratch_shapes=[
            pltpu.VMEM((2, 1, rows), jnp.float32),
            pltpu.VMEM((2, 1, rows), jnp.float32),
            pltpu.VMEM((2, pair, rows), jnp.float32),
        ],
    )
    return pl.pallas_call(
        functools.partial(attention_kernel, n_blocks),
        grid_spec=grid_spec,
        out_shape=jax.ShapeDtypeStruct((rows, width), jnp.bfloat16),
        cost_estimate=pl.CostEstimate(
            flops=12 * rows * rows * width * 4,
            transcendentals=rows * rows * HEADS * 4,
            bytes_accessed=2 * rows * width * (2 * n_blocks + 2),
        ),
    )(mask, q, *blocks)


def spread_kernel(x_size, lists_ref, lengths_ref, q_ref, kv, packed,
                  ctx_ref, up_full, down_full, out_full,
                  slots, q_t, m_scr, l_scr, acc_scr, zbuf,
                  send_sems, recv_sems, local_sems, kv_send, kv_recv, z_send, z_recv):
    blk = lax.axis_index("blk")
    head = lax.axis_index("head")
    bend = lax.axis_index("bend")
    hi, x = blk // x_size, blk % x_size
    c = bend % 2
    left = (hi * x_size + (x + x_size - 1) % x_size, head, bend)
    right = (hi * x_size + (x + 1) % x_size, head, bend)
    partner = (blk, head, bend + 1 - 2 * c)
    n_head = lax.axis_size("head")
    n_ring = lax.axis_size("blk") * n_head
    me = blk * n_head + head
    ring_right = ((me + 1) % n_ring // n_head, (me + 1) % n_head, bend)
    ring_left = ((me + n_ring - 1) % n_ring // n_head, (me + n_ring - 1) % n_head, bend)
    z_right = (blk, (head + 1) % n_head, bend)
    z_left = (blk, (head + n_head - 1) % n_head, bend)
    piece_rows = packed.shape[0] // 3
    up_z = zbuf.at[:, pl.ds(piece_rows, piece_rows)]
    down_z = zbuf.at[:, pl.ds(2 * piece_rows, piece_rows)]
    out_z = zbuf.at[:, pl.ds(0, piece_rows)]
    p_own = x * 2 + c
    p_left = ((x + x_size - 1) % x_size) * 2 + c
    p_right = ((x + 1) % x_size) * 2 + c
    p_far = ((x + 2) % x_size) * 2 + c
    width = packed.shape[1]
    heads = zbuf.shape[0]
    pair = 2 * HD
    n_pairs = q_ref.shape[1] // pair
    scale = 1.0 / HD**0.5

    live = lengths_ref[0]
    biases = []
    for off in [0] + [s * dist for dist in range(1, REACH + 1) for s in (-1, 1)]:
        block_id = (me + off + n_ring) % n_ring
        listed = lists_ref[0, 0] == block_id
        for i in range(1, LIST):
            listed = listed | ((lists_ref[0, i] == block_id) & (i < live))
        biases.append(jnp.where(listed, jnp.float32(0.0), jnp.float32(-1e30)))

    barrier = pltpu.get_barrier_semaphore()
    for dev in (left, right, partner, ring_left, ring_right, z_left, z_right):
        pl.semaphore_signal(barrier, inc=1, device_id=dev, device_id_type=MESH)
    pl.semaphore_wait(barrier, 7)

    def z_send_to(src_head, k, dev, part=None):
        if part is None:
            rows_sel = slice(None)
        else:
            rows_sel = pl.ds(part * (3 * piece_rows // 2), 3 * piece_rows // 2)
        src = packed if src_head is None else zbuf.at[src_head]
        dst_head = head if src_head is None else src_head
        copy = pltpu.make_async_remote_copy(
            src_ref=src.at[rows_sel], dst_ref=zbuf.at[dst_head, rows_sel],
            send_sem=z_send.at[k], recv_sem=z_recv.at[k], device_id=dev, device_id_type=MESH)
        copy.start()
        return copy

    half_cols = q_ref.shape[1] // 2

    def kv_send_to(src, slot, dev):
        copies = []
        for part in range(2):
            cols = pl.ds(part * half_cols, half_cols)
            copy = pltpu.make_async_remote_copy(
                src_ref=src.at[:, :, cols], dst_ref=slots.at[slot, :, :, cols],
                send_sem=kv_send.at[2 * slot + part], recv_sem=kv_recv.at[2 * slot + part],
                device_id=dev, device_id_type=MESH)
            copy.start()
            copies.append(copy)
        return copies

    def up_at(p, part=None):
        cols = pl.ds(pl.multiple_of((p // 2) * width, 128), width)
        if part is None:
            return up_full.at[:, c, :, cols]
        return up_full.at[pl.ds(part * (heads // 2), heads // 2), c, :, cols]

    def down_at(p, part=None):
        if part is None:
            return down_full.at[:, p]
        return down_full.at[pl.ds(part * (heads // 2), heads // 2), p]

    def send(src, dst, k, dev):
        copy = pltpu.make_async_remote_copy(
            src_ref=src, dst_ref=dst, send_sem=send_sems.at[k], recv_sem=recv_sems.at[k],
            device_id=dev, device_id_type=MESH)
        copy.start()
        return copy

    kv_sent = [kv_send_to(kv, 0, ring_right), kv_send_to(kv, 1, ring_left)]
    own_z = pltpu.make_async_copy(packed, zbuf.at[head], local_sems.at[3])
    own_z.start()
    z_sent = [z_send_to(None, 0, z_right), z_send_to(None, 1, z_left)]

    first = lax.broadcasted_iota(jnp.int32, (pair, q_ref.shape[0]), 0) < HD
    for p in range(n_pairs):
        qp = q_ref[:, p * pair:(p + 1) * pair].T
        q_t[2 * p] = jnp.where(first, qp, jnp.zeros_like(qp))
        q_t[2 * p + 1] = jnp.where(first, jnp.zeros_like(qp), qp)
    m_scr[...] = jnp.full(m_scr.shape, -jnp.inf, jnp.float32)
    l_scr[...] = jnp.zeros(l_scr.shape, jnp.float32)
    acc_scr[...] = jnp.zeros(acc_scr.shape, jnp.float32)

    def absorb(block, bias, lo=0, hi_pair=None):
        def one_pair(p, carry):
            cols = pl.ds(pl.multiple_of(p * pair, pair), pair)
            k = block[0, :, cols]
            v_t = block[1, :, cols].T
            for hh in range(2):
                h = 2 * p + hh
                s_t = jnp.dot(k, q_t[h], preferred_element_type=jnp.float32) * scale + bias
                m_old = m_scr[h]
                m_new = jnp.maximum(m_old, jnp.max(s_t, axis=0, keepdims=True))
                alpha = jnp.exp(m_old - m_new)
                w_t = jnp.exp(s_t - m_new)
                l_scr[h] = alpha * l_scr[h] + jnp.sum(w_t, axis=0, keepdims=True)
                acc_scr[h] = alpha * acc_scr[h] + jnp.dot(
                    v_t, w_t.astype(jnp.bfloat16), preferred_element_type=jnp.float32)
                m_scr[h] = m_new
            return carry
        lax.fori_loop(lo, n_pairs if hi_pair is None else hi_pair, one_pair, 0)

    def wait_kv(slot, part):
        kv_sent[slot][part].wait_recv()

    absorb(kv, biases[0])

    for dist in range(1, n_head // 2):
        z_sent[2 * dist - 2].wait_recv()
        z_sent[2 * dist - 1].wait_recv()
        from_left = (head + n_head - dist) % n_head
        from_right = (head + dist) % n_head
        if dist < n_head // 2 - 1:
            z_sent += [z_send_to(from_left, 2 * dist, z_right),
                       z_send_to(from_right, 2 * dist + 1, z_left)]
        else:
            z_sent += [z_send_to(from_left, 2 * dist, z_right, 0),
                       z_send_to(from_right, 2 * dist + 1, z_left, 1)]
        if dist == 1:
            for slot in (0, 1):
                wait_kv(slot, 0)
                wait_kv(slot, 1)
            kv_sent += [kv_send_to(slots.at[0], 2, ring_right),
                        kv_send_to(slots.at[1], 3, ring_left)]
    z_sent[-2].wait_recv()
    z_sent[-1].wait_recv()
    own_z.wait()

    local = [
        pltpu.make_async_copy(up_z, up_at(p_own), local_sems.at[0]),
        pltpu.make_async_copy(down_z, down_at(p_own), local_sems.at[1]),
        pltpu.make_async_copy(out_z, out_full.at[:, c], local_sems.at[2]),
    ]
    for copy in local:
        copy.start()
    a_up_r = send(up_z, up_at(p_own), 0, right)
    a_up_l = send(up_z, up_at(p_own), 1, left)
    a_dn_r = send(down_z, down_at(p_own), 2, right)
    a_dn_l = send(down_z, down_at(p_own), 3, left)
    sent = [a_up_r, a_up_l, a_dn_r, a_dn_l]
    sent += [
        send(out_z, out_full.at[:, c], 4, partner),
        send(up_z, up_at(p_own), 5, partner),
        send(down_z, down_at(p_own), 6, partner),
    ]
    a_up_r.wait_recv()
    a_dn_r.wait_recv()
    b_up_r = send(up_at(p_left, 0), up_at(p_left, 0), 7, right)
    b_dn_r = send(down_at(p_left, 0), down_at(p_left, 0), 8, right)
    sent += [b_up_r, b_dn_r]
    sent += [send(up_at(p_left), up_at(p_left), 9, partner),
             send(down_at(p_left), down_at(p_left), 10, partner)]
    a_up_l.wait_recv()
    a_dn_l.wait_recv()
    b_up_l = send(up_at(p_right, 1), up_at(p_right, 1), 11, left)
    b_dn_l = send(down_at(p_right, 1), down_at(p_right, 1), 12, left)
    sent += [b_up_l, b_dn_l]
    sent += [send(up_at(p_right), up_at(p_right), 13, partner),
             send(down_at(p_right), down_at(p_right), 14, partner)]

    for slot in (2, 3):
        wait_kv(slot, 0)
        wait_kv(slot, 1)
    kv_sent += [kv_send_to(slots.at[2], 4, ring_right), kv_send_to(slots.at[3], 5, ring_left)]

    b_up_r.wait_recv()
    b_dn_r.wait_recv()
    sent += [send(up_at(p_far, 0), up_at(p_far, 0), 15, partner),
             send(down_at(p_far, 0), down_at(p_far, 0), 16, partner)]
    b_up_l.wait_recv()
    b_dn_l.wait_recv()
    sent += [send(up_at(p_far, 1), up_at(p_far, 1), 17, partner),
             send(down_at(p_far, 1), down_at(p_far, 1), 18, partner)]

    absorb(slots.at[0], biases[1])
    absorb(slots.at[1], biases[2])
    absorb(slots.at[2], biases[3])
    absorb(slots.at[3], biases[4])

    half_pairs = n_pairs // 2
    wait_kv(4, 0)
    absorb(slots.at[4], biases[5], 0, half_pairs)
    wait_kv(5, 0)
    absorb(slots.at[5], biases[6], 0, half_pairs)
    wait_kv(4, 1)
    absorb(slots.at[4], biases[5], half_pairs, n_pairs)
    wait_kv(5, 1)
    absorb(slots.at[5], biases[6], half_pairs, n_pairs)

    row = lax.broadcasted_iota(jnp.int32, (pair, q_ref.shape[0]), 0) < HD

    def write_pair(p, carry):
        out_t = jnp.where(row, acc_scr[2 * p] / l_scr[2 * p], acc_scr[2 * p + 1] / l_scr[2 * p + 1])
        ctx_ref[:, pl.ds(pl.multiple_of(p * pair, pair), pair)] = out_t.T.astype(ctx_ref.dtype)
        return carry
    lax.fori_loop(0, n_pairs, write_pair, 0)

    for k in (4, 5, 6, 9, 10, 13, 14, 15, 16, 17, 18):
        sent[k].wait_recv()
    for copy in sent + [c for pair_ in kv_sent for c in pair_] + z_sent:
        copy.wait_send()
    for copy in local:
        copy.wait()


def exchange(lists, lengths, q, kv, packed, n_heads, x_size):
    piece_rows, d = packed.shape[0] // 3, packed.shape[1]
    n_rows = q.shape[0]
    n_pieces = 2 * x_size
    any_spec = pl.BlockSpec(memory_space=pl.ANY)
    vmem_spec = pl.BlockSpec(memory_space=pltpu.VMEM)
    return pl.pallas_call(
        functools.partial(spread_kernel, x_size),
        out_shape=(
            jax.ShapeDtypeStruct(q.shape, jnp.bfloat16),
            jax.ShapeDtypeStruct((n_heads, 2, piece_rows, x_size * d), packed.dtype),
            jax.ShapeDtypeStruct((n_heads, n_pieces, piece_rows, d), packed.dtype),
            jax.ShapeDtypeStruct((n_heads, 2, piece_rows, d), packed.dtype),
        ),
        in_specs=[pl.BlockSpec(memory_space=pltpu.SMEM)] * 2 + [vmem_spec] * 3,
        out_specs=(vmem_spec, any_spec, any_spec, any_spec),
        scratch_shapes=[
            pltpu.VMEM((2 * REACH,) + kv.shape, kv.dtype),
            pltpu.VMEM((HEADS, 2 * HD, n_rows), jnp.bfloat16),
            pltpu.VMEM((HEADS, 1, n_rows), jnp.float32),
            pltpu.VMEM((HEADS, 1, n_rows), jnp.float32),
            pltpu.VMEM((HEADS, 2 * HD, n_rows), jnp.float32),
            pltpu.VMEM((n_heads,) + packed.shape, packed.dtype),
            pltpu.SemaphoreType.DMA((19,)),
            pltpu.SemaphoreType.DMA((19,)),
            pltpu.SemaphoreType.DMA((4,)),
            pltpu.SemaphoreType.DMA((4 * REACH,)),
            pltpu.SemaphoreType.DMA((4 * REACH,)),
            pltpu.SemaphoreType.DMA((n_heads,)),
            pltpu.SemaphoreType.DMA((n_heads,)),
        ],
        compiler_params=pltpu.CompilerParams(
            collective_id=1, has_side_effects=True, vmem_limit_bytes=48 * 1024 * 1024),
        cost_estimate=pl.CostEstimate(
            flops=6 * n_rows * n_rows * q.shape[1] * (2 * REACH + 1),
            transcendentals=n_rows * n_rows * HEADS * (2 * REACH + 1),
            bytes_accessed=2 * n_heads * piece_rows * d * (3 * n_pieces),
        ),
    )(lists, lengths, q, kv, packed)


def shards(
    queries,
    keys_values,
    surface,
    out_weight,
    up_weight,
    down_weight,
    norm_gain,
    block_lists,
    list_lengths,
):
    row_count, feature_width = queries.shape
    loop_size = lax.axis_size(("blk", "head"))
    blk_size = lax.axis_size("blk")
    bend_size = lax.axis_size("bend")
    x_size = 4
    own_index = lax.axis_index(("blk", "head"))
    x = lax.axis_index("blk") % x_size
    core = lax.axis_index("bend") % 2
    piece = x * 2 + core
    n_pieces = 2 * x_size

    head_size = lax.axis_size("head")
    d = feature_width
    out_rows = out_weight.shape[0] // 2
    down_rows = down_weight.shape[0] // n_pieces
    up_rows = up_weight.shape[0] // 2
    packed = jnp.concatenate([
        lax.dynamic_slice_in_dim(out_weight, core * out_rows, out_rows, axis=0),
        lax.dynamic_slice(up_weight, (core * up_rows, x * d), (up_rows, d)),
        lax.dynamic_slice_in_dim(down_weight, piece * down_rows, down_rows, axis=0),
    ], axis=0)
    context, up_full, down_full, out_full = exchange(
        block_lists, list_lengths, queries, keys_values, packed, head_size, x_size)
    out_full = out_full.reshape(d, d)
    up_full = up_full.reshape(d, -1)
    down_full = down_full.reshape(-1, d)

    hidden = surface.astype(jnp.float32) + jnp.dot(
        context, out_full, preferred_element_type=jnp.float32)
    mean_square = jnp.mean(hidden * hidden, axis=1, keepdims=True)
    normed = (hidden * lax.rsqrt(mean_square + 1e-05) * norm_gain[None, :]).astype(jnp.bfloat16)
    pre_gelu = jnp.dot(normed, up_full, preferred_element_type=jnp.float32)
    activated = jax.nn.gelu(pre_gelu, approximate=True).astype(jnp.bfloat16)
    mixed_out = hidden + jnp.dot(activated, down_full, preferred_element_type=jnp.float32)
    return mixed_out.astype(jnp.bfloat16)


def solution(mesh):
    return jax.shard_map(
        shards,
        mesh=mesh,
        in_specs=(
            P(("bend", "blk", "head"), None),
            P(None, ("bend", "blk", "head"), None),
            P(("bend", "blk", "head"), None),
            P("head", None),
            P("head", None),
            P("head", None),
            P(),
            P(("bend", "blk", "head"), None),
            P(("bend", "blk", "head")),
        ),
        out_specs=P(("bend", "blk", "head"), None),
        check_vma=False,
    )
```

```python
import functools

import jax
import jax.numpy as jnp
from jax import lax
from jax.experimental import pallas as pl
from jax.experimental.pallas import tpu as pltpu
from jax.sharding import PartitionSpec as P

HEADS = 12
HD = 64
LIST = 4
REACH = 3
MESH = pl.DeviceIdType.MESH


def ring_shift(block, axis, size, distance):
    route = [(i, (i + distance) % size) for i in range(size)]
    return lax.ppermute(block, axis, route)


def x_shift(block, blk_size, x_size, distance):
    route = []
    for i in range(blk_size):
        hi, x = divmod(i, x_size)
        route.append((i, hi * x_size + (x + distance) % x_size))
    return lax.ppermute(block, "blk", route)


def core_swap(block, bend_size):
    route = [(i, i ^ 1) for i in range(bend_size)]
    return lax.ppermute(block, "bend", route)


def attention_kernel(n_blocks, mask_ref, q_ref, *refs):
    kv_refs = refs[:n_blocks]
    o_ref = refs[n_blocks]
    m_scr, l_scr, acc_scr = refs[n_blocks + 1:]
    scale = 1.0 / HD**0.5
    q_t = q_ref[...].T
    first = lax.broadcasted_iota(jnp.int32, q_t.shape, 0) < HD
    zero = jnp.zeros_like(q_t)
    halves = (jnp.where(first, q_t, zero), jnp.where(first, zero, q_t))
    for hh in range(2):
        m_scr[hh] = jnp.full(m_scr.shape[1:], -jnp.inf, jnp.float32)
        l_scr[hh] = jnp.zeros(l_scr.shape[1:], jnp.float32)
        acc_scr[hh] = jnp.zeros(acc_scr.shape[1:], jnp.float32)
    for j in range(n_blocks):
        @pl.when(mask_ref[j] > 0)
        def _():
            k = kv_refs[j][0]
            for hh in range(2):
                s_t = jnp.dot(k, halves[hh], preferred_element_type=jnp.float32) * scale
                m_scr[hh] = jnp.maximum(m_scr[hh], jnp.max(s_t, axis=0, keepdims=True))
    for j in range(n_blocks):
        @pl.when(mask_ref[j] > 0)
        def _():
            k = kv_refs[j][0]
            v_t = kv_refs[j][1].T
            for hh in range(2):
                s_t = jnp.dot(k, halves[hh], preferred_element_type=jnp.float32) * scale
                w_t = jnp.exp(s_t - m_scr[hh])
                l_scr[hh] += jnp.sum(w_t, axis=0, keepdims=True)
                acc_scr[hh] += jnp.dot(v_t, w_t.astype(jnp.bfloat16),
                                       preferred_element_type=jnp.float32)
    lane = lax.broadcasted_iota(jnp.int32, acc_scr.shape[1:], 0) < HD
    out_t = jnp.where(lane, acc_scr[0] / l_scr[0], acc_scr[1] / l_scr[1])
    o_ref[...] = out_t.T.astype(o_ref.dtype)


def attend(mask, q, blocks):
    rows, width = q.shape
    n_blocks = len(blocks)
    pair = 2 * HD
    grid_spec = pltpu.PrefetchScalarGridSpec(
        num_scalar_prefetch=1,
        grid=(width // pair,),
        in_specs=[pl.BlockSpec((rows, pair), lambda p, m: (0, p))]
        + [pl.BlockSpec((2, rows, pair), lambda p, m: (0, 0, p))] * n_blocks,
        out_specs=pl.BlockSpec((rows, pair), lambda p, m: (0, p)),
        scratch_shapes=[
            pltpu.VMEM((2, 1, rows), jnp.float32),
            pltpu.VMEM((2, 1, rows), jnp.float32),
            pltpu.VMEM((2, pair, rows), jnp.float32),
        ],
    )
    return pl.pallas_call(
        functools.partial(attention_kernel, n_blocks),
        grid_spec=grid_spec,
        out_shape=jax.ShapeDtypeStruct((rows, width), jnp.bfloat16),
        cost_estimate=pl.CostEstimate(
            flops=12 * rows * rows * width * 4,
            transcendentals=rows * rows * HEADS * 4,
            bytes_accessed=2 * rows * width * (2 * n_blocks + 2),
        ),
    )(mask, q, *blocks)


def spread_kernel(x_size, lists_ref, lengths_ref, q_ref, kv, packed,
                  ctx_ref, up_full, down_full, out_full,
                  slots, q_t, m_scr, l_scr, acc_scr, zbuf,
                  send_sems, recv_sems, local_sems, kv_send, kv_recv, z_send, z_recv):
    blk = lax.axis_index("blk")
    head = lax.axis_index("head")
    bend = lax.axis_index("bend")
    hi, x = blk // x_size, blk % x_size
    c = bend % 2
    left = (hi * x_size + (x + x_size - 1) % x_size, head, bend)
    right = (hi * x_size + (x + 1) % x_size, head, bend)
    partner = (blk, head, bend + 1 - 2 * c)
    n_head = lax.axis_size("head")
    n_ring = lax.axis_size("blk") * n_head
    me = blk * n_head + head
    ring_right = ((me + 1) % n_ring // n_head, (me + 1) % n_head, bend)
    ring_left = ((me + n_ring - 1) % n_ring // n_head, (me + n_ring - 1) % n_head, bend)
    z_right = (blk, (head + 1) % n_head, bend)
    z_left = (blk, (head + n_head - 1) % n_head, bend)
    piece_rows = packed.shape[0] // 3
    up_z = zbuf.at[:, pl.ds(piece_rows, piece_rows)]
    down_z = zbuf.at[:, pl.ds(2 * piece_rows, piece_rows)]
    out_z = zbuf.at[:, pl.ds(0, piece_rows)]
    p_own = x * 2 + c
    p_left = ((x + x_size - 1) % x_size) * 2 + c
    p_right = ((x + 1) % x_size) * 2 + c
    p_far = ((x + 2) % x_size) * 2 + c
    width = packed.shape[1]
    heads = zbuf.shape[0]
    pair = 2 * HD
    n_pairs = q_ref.shape[1] // pair
    scale = 1.0 / HD**0.5

    live = lengths_ref[0]
    biases = []
    for off in [0] + [s * dist for dist in range(1, REACH + 1) for s in (-1, 1)]:
        block_id = (me + off + n_ring) % n_ring
        listed = lists_ref[0, 0] == block_id
        for i in range(1, LIST):
            listed = listed | ((lists_ref[0, i] == block_id) & (i < live))
        biases.append(jnp.where(listed, jnp.float32(0.0), jnp.float32(-1e30)))

    barrier = pltpu.get_barrier_semaphore()
    for dev in (left, right, partner, ring_left, ring_right, z_left, z_right):
        pl.semaphore_signal(barrier, inc=1, device_id=dev, device_id_type=MESH)
    pl.semaphore_wait(barrier, 7)

    def z_send_to(src_head, k, dev, part=None):
        if part is None:
            rows_sel = slice(None)
        else:
            rows_sel = pl.ds(part * (3 * piece_rows // 2), 3 * piece_rows // 2)
        src = packed if src_head is None else zbuf.at[src_head]
        dst_head = head if src_head is None else src_head
        copy = pltpu.make_async_remote_copy(
            src_ref=src.at[rows_sel], dst_ref=zbuf.at[dst_head, rows_sel],
            send_sem=z_send.at[k], recv_sem=z_recv.at[k], device_id=dev, device_id_type=MESH)
        copy.start()
        return copy

    half_cols = q_ref.shape[1] // 2

    def kv_send_to(src, slot, dev):
        copies = []
        for part in range(2):
            cols = pl.ds(part * half_cols, half_cols)
            copy = pltpu.make_async_remote_copy(
                src_ref=src.at[:, :, cols], dst_ref=slots.at[slot, :, :, cols],
                send_sem=kv_send.at[2 * slot + part], recv_sem=kv_recv.at[2 * slot + part],
                device_id=dev, device_id_type=MESH)
            copy.start()
            copies.append(copy)
        return copies

    def up_at(p, part=None):
        cols = pl.ds(pl.multiple_of((p // 2) * width, 128), width)
        if part is None:
            return up_full.at[:, c, :, cols]
        return up_full.at[pl.ds(part * (heads // 2), heads // 2), c, :, cols]

    def down_at(p, part=None):
        if part is None:
            return down_full.at[:, p]
        return down_full.at[pl.ds(part * (heads // 2), heads // 2), p]

    def send(src, dst, k, dev):
        copy = pltpu.make_async_remote_copy(
            src_ref=src, dst_ref=dst, send_sem=send_sems.at[k], recv_sem=recv_sems.at[k],
            device_id=dev, device_id_type=MESH)
        copy.start()
        return copy

    kv_sent = [kv_send_to(kv, 0, ring_right), kv_send_to(kv, 1, ring_left)]
    own_z = pltpu.make_async_copy(packed, zbuf.at[head], local_sems.at[3])
    own_z.start()
    z_sent = [z_send_to(None, 0, z_right), z_send_to(None, 1, z_left)]

    first = lax.broadcasted_iota(jnp.int32, (pair, q_ref.shape[0]), 0) < HD
    for p in range(n_pairs):
        qp = q_ref[:, p * pair:(p + 1) * pair].T
        q_t[2 * p] = jnp.where(first, qp, jnp.zeros_like(qp))
        q_t[2 * p + 1] = jnp.where(first, jnp.zeros_like(qp), qp)
    m_scr[...] = jnp.full(m_scr.shape, -jnp.inf, jnp.float32)
    l_scr[...] = jnp.zeros(l_scr.shape, jnp.float32)
    acc_scr[...] = jnp.zeros(acc_scr.shape, jnp.float32)

    def absorb(block, bias, lo=0, hi_pair=None):
        def one_pair(p, carry):
            cols = pl.ds(pl.multiple_of(p * pair, pair), pair)
            k = block[0, :, cols]
            v_t = block[1, :, cols].T
            for hh in range(2):
                h = 2 * p + hh
                s_t = jnp.dot(k, q_t[h], preferred_element_type=jnp.float32) * scale + bias
                m_old = m_scr[h]
                m_new = jnp.maximum(m_old, jnp.max(s_t, axis=0, keepdims=True))
                alpha = jnp.exp(m_old - m_new)
                w_t = jnp.exp(s_t - m_new)
                l_scr[h] = alpha * l_scr[h] + jnp.sum(w_t, axis=0, keepdims=True)
                acc_scr[h] = alpha * acc_scr[h] + jnp.dot(
                    v_t, w_t.astype(jnp.bfloat16), preferred_element_type=jnp.float32)
                m_scr[h] = m_new
            return carry
        lax.fori_loop(lo, n_pairs if hi_pair is None else hi_pair, one_pair, 0)

    def wait_kv(slot, part):
        kv_sent[slot][part].wait_recv()

    absorb(kv, biases[0])

    for dist in range(1, n_head // 2):
        z_sent[2 * dist - 2].wait_recv()
        z_sent[2 * dist - 1].wait_recv()
        from_left = (head + n_head - dist) % n_head
        from_right = (head + dist) % n_head
        if dist < n_head // 2 - 1:
            z_sent += [z_send_to(from_left, 2 * dist, z_right),
                       z_send_to(from_right, 2 * dist + 1, z_left)]
        else:
            z_sent += [z_send_to(from_left, 2 * dist, z_right, 0),
                       z_send_to(from_right, 2 * dist + 1, z_left, 1)]
        if dist == 1:
            for slot in (0, 1):
                wait_kv(slot, 0)
                wait_kv(slot, 1)
            kv_sent += [kv_send_to(slots.at[0], 2, ring_right),
                        kv_send_to(slots.at[1], 3, ring_left)]
            absorb(slots.at[0], biases[1])
            absorb(slots.at[1], biases[2])
    z_sent[-2].wait_recv()
    z_sent[-1].wait_recv()
    own_z.wait()

    local = [
        pltpu.make_async_copy(up_z, up_at(p_own), local_sems.at[0]),
        pltpu.make_async_copy(down_z, down_at(p_own), local_sems.at[1]),
        pltpu.make_async_copy(out_z, out_full.at[:, c], local_sems.at[2]),
    ]
    for copy in local:
        copy.start()
    a_up_r = send(up_z, up_at(p_own), 0, right)
    a_up_l = send(up_z, up_at(p_own), 1, left)
    a_dn_r = send(down_z, down_at(p_own), 2, right)
    a_dn_l = send(down_z, down_at(p_own), 3, left)
    sent = [a_up_r, a_up_l, a_dn_r, a_dn_l]
    sent += [
        send(out_z, out_full.at[:, c], 4, partner),
        send(up_z, up_at(p_own), 5, partner),
        send(down_z, down_at(p_own), 6, partner),
    ]
    a_up_r.wait_recv()
    a_dn_r.wait_recv()
    b_up_r = send(up_at(p_left, 0), up_at(p_left, 0), 7, right)
    b_dn_r = send(down_at(p_left, 0), down_at(p_left, 0), 8, right)
    sent += [b_up_r, b_dn_r]
    sent += [send(up_at(p_left), up_at(p_left), 9, partner),
             send(down_at(p_left), down_at(p_left), 10, partner)]
    a_up_l.wait_recv()
    a_dn_l.wait_recv()
    b_up_l = send(up_at(p_right, 1), up_at(p_right, 1), 11, left)
    b_dn_l = send(down_at(p_right, 1), down_at(p_right, 1), 12, left)
    sent += [b_up_l, b_dn_l]
    sent += [send(up_at(p_right), up_at(p_right), 13, partner),
             send(down_at(p_right), down_at(p_right), 14, partner)]


    for slot in (2, 3):
        wait_kv(slot, 0)
        wait_kv(slot, 1)
    kv_sent += [kv_send_to(slots.at[2], 4, ring_right), kv_send_to(slots.at[3], 5, ring_left)]
    b_up_r.wait_recv()
    b_dn_r.wait_recv()
    sent += [send(up_at(p_far, 0), up_at(p_far, 0), 15, partner),
             send(down_at(p_far, 0), down_at(p_far, 0), 16, partner)]
    b_up_l.wait_recv()
    b_dn_l.wait_recv()
    sent += [send(up_at(p_far, 1), up_at(p_far, 1), 17, partner),
             send(down_at(p_far, 1), down_at(p_far, 1), 18, partner)]

    absorb(slots.at[2], biases[3])
    absorb(slots.at[3], biases[4])

    half_pairs = n_pairs // 2
    wait_kv(4, 0)
    absorb(slots.at[4], biases[5], 0, half_pairs)
    wait_kv(5, 0)
    absorb(slots.at[5], biases[6], 0, half_pairs)
    wait_kv(4, 1)
    absorb(slots.at[4], biases[5], half_pairs, n_pairs)
    wait_kv(5, 1)
    absorb(slots.at[5], biases[6], half_pairs, n_pairs)

    row = lax.broadcasted_iota(jnp.int32, (pair, q_ref.shape[0]), 0) < HD

    def write_pair(p, carry):
        out_t = jnp.where(row, acc_scr[2 * p] / l_scr[2 * p], acc_scr[2 * p + 1] / l_scr[2 * p + 1])
        ctx_ref[:, pl.ds(pl.multiple_of(p * pair, pair), pair)] = out_t.T.astype(ctx_ref.dtype)
        return carry
    lax.fori_loop(0, n_pairs, write_pair, 0)

    for k in (4, 5, 6, 9, 10, 13, 14, 15, 16, 17, 18):
        sent[k].wait_recv()
    for copy in sent + [c for pair_ in kv_sent for c in pair_] + z_sent:
        copy.wait_send()
    for copy in local:
        copy.wait()


def exchange(lists, lengths, q, kv, packed, n_heads, x_size):
    piece_rows, d = packed.shape[0] // 3, packed.shape[1]
    n_rows = q.shape[0]
    n_pieces = 2 * x_size
    any_spec = pl.BlockSpec(memory_space=pl.ANY)
    vmem_spec = pl.BlockSpec(memory_space=pltpu.VMEM)
    return pl.pallas_call(
        functools.partial(spread_kernel, x_size),
        out_shape=(
            jax.ShapeDtypeStruct(q.shape, jnp.bfloat16),
            jax.ShapeDtypeStruct((n_heads, 2, piece_rows, x_size * d), packed.dtype),
            jax.ShapeDtypeStruct((n_heads, n_pieces, piece_rows, d), packed.dtype),
            jax.ShapeDtypeStruct((n_heads, 2, piece_rows, d), packed.dtype),
        ),
        in_specs=[pl.BlockSpec(memory_space=pltpu.SMEM)] * 2 + [vmem_spec] * 3,
        out_specs=(vmem_spec, any_spec, any_spec, any_spec),
        scratch_shapes=[
            pltpu.VMEM((2 * REACH,) + kv.shape, kv.dtype),
            pltpu.VMEM((HEADS, 2 * HD, n_rows), jnp.bfloat16),
            pltpu.VMEM((HEADS, 1, n_rows), jnp.float32),
            pltpu.VMEM((HEADS, 1, n_rows), jnp.float32),
            pltpu.VMEM((HEADS, 2 * HD, n_rows), jnp.float32),
            pltpu.VMEM((n_heads,) + packed.shape, packed.dtype),
            pltpu.SemaphoreType.DMA((19,)),
            pltpu.SemaphoreType.DMA((19,)),
            pltpu.SemaphoreType.DMA((4,)),
            pltpu.SemaphoreType.DMA((4 * REACH,)),
            pltpu.SemaphoreType.DMA((4 * REACH,)),
            pltpu.SemaphoreType.DMA((n_heads,)),
            pltpu.SemaphoreType.DMA((n_heads,)),
        ],
        compiler_params=pltpu.CompilerParams(
            collective_id=1, has_side_effects=True, vmem_limit_bytes=48 * 1024 * 1024),
        cost_estimate=pl.CostEstimate(
            flops=6 * n_rows * n_rows * q.shape[1] * (2 * REACH + 1),
            transcendentals=n_rows * n_rows * HEADS * (2 * REACH + 1),
            bytes_accessed=2 * n_heads * piece_rows * d * (3 * n_pieces),
        ),
    )(lists, lengths, q, kv, packed)


def shards(
    queries,
    keys_values,
    surface,
    out_weight,
    up_weight,
    down_weight,
    norm_gain,
    block_lists,
    list_lengths,
):
    row_count, feature_width = queries.shape
    loop_size = lax.axis_size(("blk", "head"))
    blk_size = lax.axis_size("blk")
    bend_size = lax.axis_size("bend")
    x_size = 4
    own_index = lax.axis_index(("blk", "head"))
    x = lax.axis_index("blk") % x_size
    core = lax.axis_index("bend") % 2
    piece = x * 2 + core
    n_pieces = 2 * x_size

    head_size = lax.axis_size("head")
    d = feature_width
    out_rows = out_weight.shape[0] // 2
    down_rows = down_weight.shape[0] // n_pieces
    up_rows = up_weight.shape[0] // 2
    packed = jnp.concatenate([
        lax.dynamic_slice_in_dim(out_weight, core * out_rows, out_rows, axis=0),
        lax.dynamic_slice(up_weight, (core * up_rows, x * d), (up_rows, d)),
        lax.dynamic_slice_in_dim(down_weight, piece * down_rows, down_rows, axis=0),
    ], axis=0)
    context, up_full, down_full, out_full = exchange(
        block_lists, list_lengths, queries, keys_values, packed, head_size, x_size)
    out_full = out_full.reshape(d, d)
    up_full = up_full.reshape(d, -1)
    down_full = down_full.reshape(-1, d)

    hidden = surface.astype(jnp.float32) + jnp.dot(
        context, out_full, preferred_element_type=jnp.float32)
    mean_square = jnp.mean(hidden * hidden, axis=1, keepdims=True)
    normed = (hidden * lax.rsqrt(mean_square + 1e-05) * norm_gain[None, :]).astype(jnp.bfloat16)
    pre_gelu = jnp.dot(normed, up_full, preferred_element_type=jnp.float32)
    activated = jax.nn.gelu(pre_gelu, approximate=True).astype(jnp.bfloat16)
    mixed_out = hidden + jnp.dot(activated, down_full, preferred_element_type=jnp.float32)
    return mixed_out.astype(jnp.bfloat16)


def solution(mesh):
    return jax.shard_map(
        shards,
        mesh=mesh,
        in_specs=(
            P(("bend", "blk", "head"), None),
            P(None, ("bend", "blk", "head"), None),
            P(("bend", "blk", "head"), None),
            P("head", None),
            P("head", None),
            P("head", None),
            P(),
            P(("bend", "blk", "head"), None),
            P(("bend", "blk", "head")),
        ),
        out_specs=P(("bend", "blk", "head"), None),
        check_vma=False,
    )
```
